32 devices in a mesh: seq: 8 (over z, core), fsdp: 4 (over y, x).
Axes of the slice: x: 2, y: 2, z: 4, core: 2. Of those that a mesh axis runs over, the one named last changes fastest.
Arguments:
- tokens: bfloat16 [8, 1024, 2048], P('fsdp', 'seq'), may hold values from -6 to 6
- attn_gain: bfloat16 [2048], P('fsdp'), may hold values from 0.25 to 1.75
- attn_shift: bfloat16 [2048], P('fsdp'), may hold values from -1.5 to 1.5
- qkv_weight: bfloat16 [2048, 6144], P('fsdp'), may hold values from -0.125 to 0.125
- qkv_bias: bfloat16 [6144], P('fsdp'), may hold values from -1.5 to 1.5
- out_weight: bfloat16 [2048, 2048], P('fsdp'), may hold values from -0.375 to 0.375
- ffn_gain: bfloat16 [2048], P('fsdp'), may hold values from 0.25 to 1.75
- ffn_shift: bfloat16 [2048], P('fsdp'), may hold values from -1.5 to 1.5
- gate_weight: bfloat16 [2048, 5632], P('fsdp'), may hold values from -0.125 to 0.125
- up_weight: bfloat16 [2048, 5632], P('fsdp'), may hold values from -0.125 to 0.125
- down_weight: bfloat16 [5632, 2048], P('fsdp'), may hold values from -0.078125 to 0.078125
- cotangent: bfloat16 [8, 1024, 2048], P('fsdp', 'seq'), may hold values from -6 to 6
Outputs:
- layer_out: bfloat16 [8, 1024, 2048], P('fsdp', 'seq')
- tokens_grad: float32 [8, 1024, 2048], P('fsdp', 'seq')
- attn_gain_grad: float32 [2048], P(('seq', 'fsdp'))
- attn_shift_grad: float32 [2048], P(('seq', 'fsdp'))
- qkv_weight_grad: float32 [2048, 6144], P('fsdp', 'seq')
- qkv_bias_grad: float32 [4096], P(('seq', 'fsdp'))
- value_bias_grad: float32 [2048], P(('seq', 'fsdp'))
- out_weight_grad: float32 [2048, 2048], P('fsdp', 'seq')
- ffn_gain_grad: float32 [2048], P(('seq', 'fsdp'))
- ffn_shift_grad: float32 [2048], P(('seq', 'fsdp'))
- gate_weight_grad: float32 [2048, 5632], P('fsdp', 'seq')
- up_weight_grad: float32 [2048, 5632], P('fsdp', 'seq')
- down_weight_grad: float32 [5632, 2048], P('fsdp', 'seq')
The draws below stay inside these ranges and needn't reach their ends.
All inputs are finite; a program needn't handle non-finite values.
Results may differ from the reference program's by a relative error of at most 0.023.
Values may be sent and summed in bfloat16 or wider, within the bound.
No kernel may reach another device: no remote copies, remote signals or barrier semaphores. Data moves between devices by JAX's collectives and lax.ppermute only.
A program may use at most 448 MiB of HBM per device.

```python
import jax
import jax.numpy as jnp
from jax import lax

D = 2048
H = 32
HD = 64
FF = 5632
ROT = 16
SEQ_LEN = 1024
SEQS_ALL = 8


def spiked(array, rng, source, target, shards_of, factor):
    owner, partner = [(jnp.arange(array.shape[dim]) // (array.shape[dim] // shards_of)).reshape([-1 if axis == dim else 1 for axis in range(array.ndim)]) for dim in (source, target)]
    chosen = jax.random.permutation(rng, shards_of)[partner]
    strong = (owner == chosen) | (owner == (partner + shards_of // 2) % shards_of)
    return jnp.where(strong, factor * array, array)


def block_levels(rng, extent, pieces, least, largest):
    def one(dim, blocks):
        heights = jax.random.uniform(jax.random.fold_in(jax.random.fold_in(rng, 6), dim), (blocks,), jnp.float32, least / len(pieces), largest / len(pieces))
        return jnp.repeat(jnp.exp(heights), extent[dim] // blocks).reshape((-1,) + (1,) * (len(extent) - dim - 1))

    factor_of = one(*pieces[0])
    for cut in pieces[1:]:
        factor_of = factor_of * one(*cut)
    return factor_of


def gaussian(stream_key, dims, scale, limit, pieces=(), kind=jnp.bfloat16):
    gain = block_levels(stream_key, dims, pieces, -0.22, 0.18) if pieces else 1.0
    result = jax.random.normal(stream_key, dims, jnp.float32) * scale * gain
    return jnp.minimum(jnp.maximum(result, -limit), limit).astype(kind)


def bell_draw_with(stream_key, shape, width, most, cuts, heavy, kind=jnp.bfloat16):
    entries = width * jax.random.normal(stream_key, shape, jnp.float32)
    if cuts:
        entries = entries * block_levels(stream_key, shape, cuts, -0.22, 0.18)
    return jnp.clip(spiked(entries, jax.random.fold_in(stream_key, 3), *heavy), -most, most).astype(kind)


def setup_inputs(seed: int = 0) -> dict:
    arg_keys = jax.random.split(jax.random.key(seed), 13)
    return {
        "tokens": gaussian(arg_keys[0], (SEQS_ALL, SEQ_LEN, D), 1.0, 6.0, ((0, 4), (1, 8))),
        "attn_gain": jnp.clip(1.0 + 0.15 * jax.random.normal(arg_keys[1], (D,), jnp.float32), 0.25, 1.75).astype(jnp.bfloat16),
        "attn_shift": gaussian(arg_keys[2], (D,), 0.3, 1.5, ((0, 4),)),
        "qkv_weight": gaussian(arg_keys[3], (D, 3 * D), D ** -0.5, 0.125, ((0, 4),)),
        "qkv_bias": gaussian(arg_keys[4], (3 * D,), 0.3, 1.5, ((0, 4),)),
        "out_weight": gaussian(arg_keys[5], (D, D), (D // 8) ** -0.5, 0.375, ((0, 4),)),
        "ffn_gain": jnp.clip(1.0 + 0.15 * jax.random.normal(arg_keys[6], (D,), jnp.float32), 0.25, 1.75).astype(jnp.bfloat16),
        "ffn_shift": gaussian(arg_keys[7], (D,), 0.3, 1.5, ((0, 4),)),
        "gate_weight": gaussian(arg_keys[8], (D, FF), D ** -0.5, 0.125, ((0, 4),)),
        "up_weight": gaussian(arg_keys[9], (D, FF), D ** -0.5, 0.125, ((0, 4),)),
        "down_weight": gaussian(arg_keys[10], (FF, D), FF ** -0.5, 0.078125, ((0, 4),)),
        "cotangent": bell_draw_with(arg_keys[11], (SEQS_ALL, SEQ_LEN, D), 1.0, 6.0, ((0, 4), (1, 8)), (1, 2, 8, 2.0)),
    }


@jax.custom_vjp
def low(v):
    return lax.optimization_barrier(v.astype(jnp.bfloat16)).astype(jnp.float32)

@jax.custom_vjp
def low_back(v):
    return v

def low_keep(v):
    return (low(v), None)

def low_pass(kept, grad):
    return (grad,)

def back_keep(v):
    return (v, None)

def back_low(kept, grad):
    return (low(grad),)
low.defvjp(low_keep, low_pass)
low_back.defvjp(back_keep, back_low)

def matmul(former, latter):
    return jnp.dot(former, latter, precision=lax.Precision.HIGHEST)

def layer_norm(inputs, gain_vec, offset):
    center = inputs - lax.optimization_barrier(jnp.mean(inputs, axis=-1, keepdims=True))
    spread = lax.optimization_barrier(jnp.mean(center * center, axis=-1, keepdims=True))
    return center * lax.rsqrt(spread + 1e-05) * gain_vec + offset

def tables(places):
    ladder = 10000.0 ** (-jnp.arange(0, ROT, 2, dtype=jnp.float32) / ROT)
    angles = places[:, None] * ladder[None, :]
    return (jnp.cos(angles), jnp.sin(angles))

def rotary(inputs, cosine, sine_tab):
    half_rot = ROT // 2
    first_half = inputs[..., :half_rot]
    second_half = inputs[..., half_rot:ROT]
    return jnp.concatenate([first_half * cosine - second_half * sine_tab, second_half * cosine + first_half * sine_tab, inputs[..., ROT:]], axis=-1)

def attention(queries, key_rows, value_rows):
    block_rows = min(512, SEQ_LEN)
    starts = (jnp.arange(SEQ_LEN // block_rows) * block_rows).astype(jnp.int32)
    columns = jnp.arange(SEQ_LEN).astype(jnp.int32)

    def one_block(row_start):
        picked = lax.dynamic_slice_in_dim(queries, row_start, block_rows, 0)
        scores = low_back(jnp.einsum('qhd,khd->hqk', picked, key_rows, precision=lax.Precision.HIGHEST) * HD ** (-0.5))
        allowed = columns[None, :] <= (row_start + jnp.arange(block_rows).astype(jnp.int32))[:, None]
        exponent = jnp.where(allowed, jnp.exp(scores), 0.0)
        probability = low(exponent / lax.optimization_barrier(jnp.sum(exponent, axis=-1, keepdims=True)))
        return jnp.einsum('hqk,khd->qhd', probability, value_rows, precision=lax.Precision.HIGHEST)
    blocks = lax.map(jax.checkpoint(one_block), starts)
    return blocks.reshape(SEQ_LEN, H * HD)

def forward(params, tokens):
    attn_gain, attn_shift, qkv_weight, qkv_bias, out_weight, ffn_gain, ffn_shift, gate_weight, up_weight, down_weight = params
    normed = low(layer_norm(tokens, attn_gain, attn_shift))
    mixed_proj = low_back(matmul(normed, qkv_weight) + qkv_bias).reshape(SEQ_LEN, 3, H, HD)
    cosine, sine_tab = tables(jnp.arange(SEQ_LEN, dtype=jnp.float32))
    cosine = cosine[:, None, :]
    sine_tab = sine_tab[:, None, :]
    queries = low_back(low(rotary(mixed_proj[:, 0], cosine, sine_tab)))
    key_rows = low_back(low(rotary(mixed_proj[:, 1], cosine, sine_tab)))
    value_rows = low_back(low(mixed_proj[:, 2]))
    attended = low_back(low(attention(queries, key_rows, value_rows)))
    middle = tokens + low_back(matmul(attended, out_weight))
    normed_two = low(layer_norm(middle, ffn_gain, ffn_shift))
    gate_proj = low_back(matmul(normed_two, gate_weight))
    upward = low_back(matmul(normed_two, up_weight))
    hidden = low(jax.nn.silu(gate_proj) * upward)
    return middle + matmul(hidden, down_weight)

def reference(tokens, attn_gain, attn_shift, qkv_weight, qkv_bias, out_weight, ffn_gain, ffn_shift, gate_weight, up_weight, down_weight, cotangent):
    params = tuple((weight_arg.astype(jnp.float32) for weight_arg in (attn_gain, attn_shift, qkv_weight, qkv_bias, out_weight, ffn_gain, ffn_shift, gate_weight, up_weight, down_weight)))

    def one_sequence(totals, inputs_pair):
        seq_tokens, seq_cotangent = inputs_pair
        result_seq, pullback = jax.vjp(forward, params, seq_tokens.astype(jnp.float32))
        weight_grads, token_grad = pullback(seq_cotangent.astype(jnp.float32))
        totals = tuple((former + latter for former, latter in zip(totals, weight_grads)))
        return (totals, (result_seq.astype(jnp.bfloat16), token_grad))
    initial = tuple((jnp.zeros_like(weight_arg) for weight_arg in params))
    totals, (layer_out, tokens_grad) = lax.scan(one_sequence, initial, (tokens, cotangent))
    return (layer_out, tokens_grad, totals[0], totals[1], totals[2], totals[3][:2 * D], totals[3][2 * D:], totals[4], totals[5], totals[6], totals[7], totals[8], totals[9])
```

```python
import functools

import jax
import jax.numpy as jnp
import numpy as np
from jax import lax
from jax.experimental import pallas as pl
from jax.experimental.pallas import tpu as pltpu
from jax.sharding import PartitionSpec as P

H = 32
HD = 64
ROT = 16
PAIR = 2 * HD
MESH_AXES = ("seq", "fsdp")


def nn(a, b):
    return lax.dot_general(a, b, (((1,), (0,)), ((), ())), preferred_element_type=jnp.float32)


def nt(a, b):
    return lax.dot_general(a, b, (((1,), (1,)), ((), ())), preferred_element_type=jnp.float32)


def tn(a, b):
    return lax.dot_general(a, b, (((0,), (0,)), ((), ())), preferred_element_type=jnp.float32)


def norm_stats(x):
    mean = jnp.mean(x, axis=-1, keepdims=True)
    center = x - mean
    var = jnp.mean(center * center, axis=-1, keepdims=True)
    r = lax.rsqrt(var + 1e-05)
    return center * r, r


def norm_back(dn, xh, r, gain):
    e = dn * gain
    return r * (
        e
        - jnp.mean(e, axis=-1, keepdims=True)
        - xh * jnp.mean(e * xh, axis=-1, keepdims=True)
    )


def rotary_tables(length):
    lane = jnp.arange(PAIR) % HD
    ladder = 10000.0 ** (-jnp.arange(0, ROT, 2, dtype=jnp.float32) / ROT)
    places = jnp.arange(length, dtype=jnp.float32)
    angles = places[:, None] * ladder[None, :]
    cosine = jnp.tile(jnp.cos(angles), (1, PAIR // (ROT // 2)))
    sine = jnp.tile(jnp.sin(angles), (1, PAIR // (ROT // 2)))
    first = lane < ROT // 2
    second = (lane >= ROT // 2) & (lane < ROT)
    turned = first | second
    cos_tab = jnp.where(turned[None, :], cosine, 1.0)
    minus = jnp.where(first[None, :], -sine, 0.0)
    plus = jnp.where(second[None, :], sine, 0.0)
    return cos_tab, minus, plus


def rotate(x, cos_tab, minus, plus):
    ahead = pltpu.roll(x, PAIR - ROT // 2, 1)
    behind = pltpu.roll(x, ROT // 2, 1)
    return x * cos_tab + ahead * minus + behind * plus


def head_lanes(x, head):
    lane = lax.broadcasted_iota(jnp.int32, x.shape, 1)
    return jnp.where((lane < HD) == (head == 0), x, jnp.zeros_like(x))


def transposed(x):
    return x.astype(jnp.float32).T.astype(x.dtype)


def causal_exp(scores, row_block, block):
    e = jnp.exp(scores)
    if row_block:
        done = e[: row_block * block]
    last = e[row_block * block :]
    key = lax.broadcasted_iota(jnp.int32, last.shape, 0)
    query = lax.broadcasted_iota(jnp.int32, last.shape, 1)
    last = jnp.where(key <= query, last, 0.0)
    return jnp.concatenate([done, last], axis=0) if row_block else last


def attend_kernel(block, mq, mk, mv, cos_ref, minus_ref, plus_ref, q_out, k_out, v_out, o_out):
    shape = q_out.shape
    length = shape[0] * shape[2]
    tabs = (cos_ref[...], minus_ref[...], plus_ref[...])
    q = rotate(mq[...].reshape(length, PAIR), *tabs).astype(jnp.bfloat16)
    k = rotate(mk[...].reshape(length, PAIR), *tabs).astype(jnp.bfloat16)
    v = mv[...].reshape(length, PAIR).astype(jnp.bfloat16)
    q_out[...] = q.reshape(shape)
    k_out[...] = k.reshape(shape)
    v_out[...] = v.reshape(shape)
    qs = q * jnp.bfloat16(HD**-0.5)
    vt = transposed(v)
    q_heads = [head_lanes(qs, h) for h in range(2)]
    rows = []
    for i in range(length // block):
        n = (i + 1) * block
        both = []
        for h in range(2):
            e = causal_exp(nt(k[:n], q_heads[h][i * block : n]), i, block)
            inv = 1.0 / jnp.sum(e, axis=0, keepdims=True)
            p = (e * inv).astype(jnp.bfloat16)
            both.append(nn(vt[h * HD : (h + 1) * HD, :n], p))
        rows.append(jnp.concatenate(both, axis=0).T)
    o_out[...] = jnp.concatenate(rows, axis=0).astype(jnp.bfloat16).reshape(shape)


def attend_back_kernel(block, q_ref, k_ref, v_ref, do_ref, cos_ref, minus_ref, plus_ref,
                       dq_out, dk_out, dv_out, dk_acc, dv_acc):
    shape = dq_out.shape
    length = shape[0] * shape[2]
    tabs = (cos_ref[...], -minus_ref[...], -plus_ref[...])
    scale = HD**-0.5
    q = q_ref[...].reshape(length, PAIR) * jnp.bfloat16(scale)
    k = k_ref[...].reshape(length, PAIR)
    v = v_ref[...].reshape(length, PAIR)
    do = do_ref[...].reshape(length, PAIR)
    kt = transposed(k)
    q_heads = [head_lanes(q, h) for h in range(2)]
    do_heads = [head_lanes(do, h) for h in range(2)]
    dk_acc[...] = jnp.zeros_like(dk_acc)
    dv_acc[...] = jnp.zeros_like(dv_acc)
    rows = []
    for i in range(length // block):
        n = (i + 1) * block
        both = []
        for h in range(2):
            q_i = q_heads[h][i * block : n]
            do_i = do_heads[h][i * block : n]
            e = causal_exp(nt(k[:n], q_i), i, block)
            p = e * (1.0 / jnp.sum(e, axis=0, keepdims=True))
            dp = nt(v[:n], do_i)
            inner = jnp.sum(p * dp, axis=0, keepdims=True)
            ds = (p * (dp - inner)).astype(jnp.bfloat16)
            dv_acc[:n] += nn(p.astype(jnp.bfloat16), do_i)
            dk_acc[:n] += nn(ds, q_i)
            both.append(nn(kt[h * HD : (h + 1) * HD, :n], ds))
        rows.append(jnp.concatenate(both, axis=0).T)
    def finish(g):
        return g.astype(jnp.bfloat16).astype(jnp.float32)

    dq = finish(jnp.concatenate(rows, axis=0) * scale)
    dq_out[...] = rotate(dq, *tabs).astype(jnp.bfloat16).reshape(shape)
    dk_out[...] = rotate(finish(dk_acc[...]), *tabs).astype(jnp.bfloat16).reshape(shape)
    dv_out[...] = dv_acc[...].astype(jnp.bfloat16).reshape(shape)


def attention_specs(parts, seqs, local_len, width):
    pairs = width // PAIR

    def spec(offset):
        return pl.BlockSpec((parts, 1, local_len, PAIR), lambda i, j: (0, i, 0, offset * pairs + j))

    length = parts * local_len
    tab = pl.BlockSpec((length, PAIR), lambda i, j: (0, 0))
    return spec, tab, (seqs, pairs), min(256, length)


def attend(m, tabs, width):
    parts, seqs, local_len, _ = m.shape
    spec, tab, grid, block = attention_specs(parts, seqs, local_len, width)
    out = jax.ShapeDtypeStruct((parts, seqs, local_len, width), jnp.bfloat16)
    work = seqs * (width // HD) * (parts * local_len) ** 2
    return pl.pallas_call(
        functools.partial(attend_kernel, block),
        grid=grid,
        in_specs=[spec(0), spec(1), spec(2), tab, tab, tab],
        out_specs=[spec(0)] * 4,
        out_shape=[out] * 4,
        compiler_params=pltpu.CompilerParams(vmem_limit_bytes=48 << 20),
        cost_estimate=pl.CostEstimate(
            flops=work * HD * 4, bytes_accessed=m.size * 4 + out.size * 8, transcendentals=work
        ),
        name="attend",
    )(m, m, m, *tabs)


def attend_back(q, k, v, do, tabs):
    parts, seqs, local_len, width = q.shape
    spec, tab, grid, block = attention_specs(parts, seqs, local_len, width)
    out = jax.ShapeDtypeStruct(q.shape, jnp.bfloat16)
    length = parts * local_len
    work = seqs * (width // HD) * length**2
    return pl.pallas_call(
        functools.partial(attend_back_kernel, block),
        grid=grid,
        in_specs=[spec(0)] * 4 + [tab] * 3,
        out_specs=[spec(0)] * 3,
        out_shape=[out] * 3,
        scratch_shapes=[pltpu.VMEM((length, PAIR), jnp.float32)] * 2,
        compiler_params=pltpu.CompilerParams(vmem_limit_bytes=48 << 20),
        cost_estimate=pl.CostEstimate(
            flops=work * HD * 10, bytes_accessed=out.size * 14, transcendentals=work
        ),
        name="attend_back",
    )(q, k, v, do, *tabs)


def third_rounds(parts):
    left = {s: [(j, (j * parts + s) // 3, (j * parts + s) % 3) for j in range(3)] for s in range(parts)}
    rounds = []
    for _ in range(3):
        owner = {}

        def place(s, seen):
            for edge in left[s]:
                d = edge[1]
                if d in seen:
                    continue
                seen.add(d)
                if d not in owner or place(owner[d][0], seen):
                    owner[d] = (s, edge)
                    return True
            return False

        for s in range(parts):
            place(s, set())
        send = [0] * parts
        slot = [0] * parts
        pairs = []
        for d, (s, edge) in owner.items():
            left[s].remove(edge)
            send[s] = edge[0]
            slot[d] = edge[2]
            pairs.append((s, d))
        rounds.append((sorted(pairs), send, slot))
    return rounds


def contiguous_thirds(block, parts, me):
    rows, _, width = block.shape
    got = []
    slots = []
    for pairs, send, slot in third_rounds(parts):
        piece = lax.dynamic_index_in_dim(block, jnp.array(send)[me], 1, keepdims=False)
        got.append(lax.ppermute(piece, "seq", pairs))
        slots.append(jnp.array(slot)[me])
    out = []
    for k in range(3):
        out.append(jnp.where(slots[0] == k, got[0], jnp.where(slots[1] == k, got[1], got[2])))
    return jnp.concatenate(out, axis=1)


def swap_blocks(block, seq_parts, fsdp_parts, me_seq):
    ratio = seq_parts // fsdp_parts
    got = []
    for r in range(ratio):
        pairs = []
        for s in range(seq_parts):
            for f in range(fsdp_parts):
                h = (r + s) % ratio
                dest = (ratio * f + h, s // ratio)
                pairs.append((s * fsdp_parts + f, dest[0] * fsdp_parts + dest[1]))
        piece = lax.dynamic_index_in_dim(block, (r + me_seq) % ratio, 1, keepdims=False)
        got.append(lax.ppermute(piece, MESH_AXES, pairs))
    out = []
    for b in range(ratio):
        r_of_b = (me_seq - b) % ratio
        pick = got[0]
        for r in range(1, ratio):
            pick = jnp.where(r_of_b == r, got[r], pick)
        out.append(pick)
    return jnp.concatenate(out, axis=0)


def on_device(
    tokens,
    attn_gain,
    attn_shift,
    qkv_weight,
    qkv_bias,
    out_weight,
    ffn_gain,
    ffn_shift,
    gate_weight,
    up_weight,
    down_weight,
    cotangent,
):
    f32, bf16 = jnp.float32, jnp.bfloat16
    seqs, local_len, width = tokens.shape
    S = lax.axis_size("seq")
    F = lax.axis_size("fsdp")
    me = lax.axis_index("seq")
    devices = S * F
    rows = seqs * local_len
    all_rows = S * rows
    head_width = width // S
    ff_rows, _ = down_weight.shape
    shard = width // F

    small = jnp.concatenate([attn_gain, attn_shift, ffn_gain, ffn_shift, qkv_bias])
    small = lax.all_gather(small, "fsdp", axis=0)
    params = [small[:, i * shard : (i + 1) * shard].reshape(width).astype(f32) for i in range(4)]
    gain1, shift1, gain2, shift2 = params
    bias = small[:, 4 * shard :].reshape(3, S, head_width).astype(f32)
    bias = lax.dynamic_index_in_dim(bias, me, 1, keepdims=False).reshape(3 * head_width)

    x_all = lax.all_gather(tokens, "seq", axis=0).reshape(all_rows, width)
    qkv_part = lax.dynamic_index_in_dim(
        qkv_weight.reshape(shard, 3, S, head_width), me, 2, keepdims=False
    ).reshape(shard, 3 * head_width)
    w_qkv = lax.all_gather(qkv_part, "fsdp", axis=0, tiled=True)
    w_out = lax.all_gather(out_weight, "fsdp", axis=0, tiled=True)
    dy_all = lax.all_gather(cotangent.reshape(rows, width), "fsdp", axis=0, tiled=True)
    w_gate = lax.all_to_all(gate_weight, "fsdp", split_axis=1, concat_axis=0, tiled=True)
    w_up = lax.all_to_all(up_weight, "fsdp", split_axis=1, concat_axis=0, tiled=True)

    tabs = rotary_tables(S * local_len)
    xh_all, _ = norm_stats(x_all.astype(f32))
    a1 = (xh_all * gain1 + shift1).astype(bf16)
    m = nn(a1, w_qkv) + bias
    q, k, v, o = attend(m.reshape(S, seqs, local_len, 3 * head_width), tabs, head_width)
    o_loc = lax.all_to_all(o, "seq", split_axis=0, concat_axis=0, tiled=True)
    o_loc = o_loc.transpose(1, 2, 0, 3).reshape(rows, width)

    x = tokens.reshape(rows, width).astype(f32)
    x1 = x + nn(o_loc, w_out)
    xh2, r2 = norm_stats(x1)
    a2 = (xh2 * gain2 + shift2).astype(bf16)
    a2_all = lax.all_gather(a2, "fsdp", axis=0, tiled=True)

    g = nn(a2_all, w_gate)
    u = nn(a2_all, w_up)
    dh = nt(dy_all, down_weight)
    sig = jax.nn.sigmoid(g)
    silu = g * sig
    hid = (silu * u).astype(bf16)
    dg = (dh * u * sig * (1.0 + g * (1.0 - sig))).astype(bf16)
    du = (dh * silu).astype(bf16)
    dn2_part = (nt(dg, w_gate) + nt(du, w_up)).astype(bf16)
    dn2 = lax.psum_scatter(dn2_part, "fsdp", scatter_dimension=0, tiled=True).astype(f32)
    down_part = nn(hid, down_weight).astype(bf16)
    down_sum = lax.psum_scatter(down_part, "fsdp", scatter_dimension=0, tiled=True)
    layer_out = (x1 + down_sum.astype(f32)).astype(bf16).reshape(tokens.shape)

    dy = cotangent.reshape(rows, width).astype(f32)
    dx1 = dy + norm_back(dn2, xh2, r2, gain2)
    ffn_gain_part = jnp.sum(dn2 * xh2, axis=0)
    ffn_shift_part = jnp.sum(dn2, axis=0)
    dxl = dx1.astype(bf16)
    do_loc = nt(dxl, w_out).astype(bf16)
    do = lax.all_to_all(
        do_loc.reshape(seqs, local_len, S, head_width).transpose(2, 0, 1, 3),
        "seq",
        split_axis=0,
        concat_axis=0,
        tiled=True,
    )

    gate_part = tn(a2_all, dg).astype(bf16)
    up_part = tn(a2_all, du).astype(bf16)
    down_grad_part = tn(hid, dy_all).astype(bf16)
    ratio = S // F
    ff_block = ff_rows // ratio

    def ffn_grad(part):
        part = lax.psum_scatter(part, "seq", scatter_dimension=0, tiled=True)
        return swap_blocks(part.reshape(-1, ratio, ff_block), S, F, me).astype(f32)

    gate_result = ffn_grad(gate_part)
    up_result = ffn_grad(up_part)
    down_result = lax.psum_scatter(
        down_grad_part, "seq", scatter_dimension=1, tiled=True
    ).astype(f32)
    out_part = tn(o_loc, dxl).astype(bf16)
    out_part = lax.psum_scatter(out_part, "seq", scatter_dimension=1, tiled=True)
    out_result = lax.psum_scatter(out_part, "fsdp", scatter_dimension=0, tiled=True).astype(f32)

    dq, dk, dv = attend_back(q, k, v, do, tabs)
    dm = jnp.concatenate([dq, dk, dv], axis=-1).reshape(all_rows, 3 * head_width)
    dn1_part = nt(dm, w_qkv).astype(bf16)
    dn1 = lax.psum_scatter(dn1_part, "seq", scatter_dimension=0, tiled=True).astype(f32)
    qkv_part_grad = tn(a1, dm).astype(bf16)
    qkv_sum = lax.psum_scatter(qkv_part_grad, "fsdp", scatter_dimension=0, tiled=True)
    qkv_result = contiguous_thirds(qkv_sum.reshape(shard, 3, head_width), S, me).astype(f32)

    bias_part = jnp.sum(dm, axis=0, dtype=f32).reshape(3, 1, head_width)
    bias_full = lax.dynamic_update_slice_in_dim(
        jnp.zeros((3, S, head_width), f32), bias_part, me, 1
    ).reshape(3 * width)
    attn_gain_part = jnp.sum(dn1_part.astype(f32) * xh_all, axis=0)
    attn_shift_part = jnp.sum(dn1_part.astype(f32), axis=0)
    small_parts = [
        attn_gain_part,
        attn_shift_part,
        bias_full[: 2 * width],
        bias_full[2 * width :],
        ffn_gain_part,
        ffn_shift_part,
    ]
    packed = jnp.concatenate([p.reshape(devices, -1) for p in small_parts], axis=1)
    packed = lax.all_to_all(packed, MESH_AXES, split_axis=0, concat_axis=0, tiled=True)
    packed = jnp.sum(packed, axis=0)
    results = []
    start = 0
    for p in small_parts:
        size = p.shape[0] // devices
        results.append(packed[start : start + size])
        start += size
    gain1_result, shift1_result, bias_result, value_result, gain2_result, shift2_result = results

    xh, r = norm_stats(x)
    tokens_grad = (dx1 + norm_back(dn1, xh, r, gain1)).reshape(tokens.shape)
    return (
        layer_out,
        tokens_grad,
        gain1_result,
        shift1_result,
        qkv_result,
        bias_result,
        value_result,
        out_result,
        gain2_result,
        shift2_result,
        gate_result,
        up_result,
        down_result,
    )


def solution(mesh):
    return jax.shard_map(
        on_device,
        mesh=mesh,
        in_specs=(
            P("fsdp", "seq", None),
            P("fsdp"),
            P("fsdp"),
            P("fsdp", None),
            P("fsdp"),
            P("fsdp", None),
            P("fsdp"),
            P("fsdp"),
            P("fsdp", None),
            P("fsdp", None),
            P("fsdp", None),
            P("fsdp", "seq", None),
        ),
        out_specs=(
            P("fsdp", "seq", None),
            P("fsdp", "seq", None),
            P(("seq", "fsdp")),
            P(("seq", "fsdp")),
            P("fsdp", "seq"),
            P(("seq", "fsdp")),
            P(("seq", "fsdp")),
            P("fsdp", "seq"),
            P(("seq", "fsdp")),
            P(("seq", "fsdp")),
            P("fsdp", "seq"),
            P("fsdp", "seq"),
            P("fsdp", "seq"),
        ),
        check_vma=False,
    )
```

```python
import functools

import jax
import jax.numpy as jnp
from jax import lax
from jax.experimental import pallas as pl
from jax.experimental.pallas import tpu as pltpu
from jax.sharding import PartitionSpec as P


HD = 64
ROT = 16
PAIR = 2 * HD
MESH_AXES = ("seq", "fsdp")


def nn(a, b):
    return lax.dot_general(a, b, (((1,), (0,)), ((), ())), preferred_element_type=jnp.float32)


def nt(a, b):
    return lax.dot_general(a, b, (((1,), (1,)), ((), ())), preferred_element_type=jnp.float32)


def tn(a, b):
    return lax.dot_general(a, b, (((0,), (0,)), ((), ())), preferred_element_type=jnp.float32)


def norm_stats(x):
    mean = jnp.mean(x, axis=-1, keepdims=True)
    center = x - mean
    var = jnp.mean(center * center, axis=-1, keepdims=True)
    r = lax.rsqrt(var + 1e-05)
    return center * r, r


def norm_back(dn, xh, r, gain):
    e = dn * gain
    return r * (
        e
        - jnp.mean(e, axis=-1, keepdims=True)
        - xh * jnp.mean(e * xh, axis=-1, keepdims=True)
    )


def rotary_tables(length):
    lane = jnp.arange(PAIR) % HD
    ladder = 10000.0 ** (-jnp.arange(0, ROT, 2, dtype=jnp.float32) / ROT)
    places = jnp.arange(length, dtype=jnp.float32)
    angles = places[:, None] * jnp.tile(ladder, PAIR // (ROT // 2))[None, :]
    first = (lane < ROT // 2)[None, :]
    second = ((lane >= ROT // 2) & (lane < ROT))[None, :]
    cos_tab = jnp.where(first | second, jnp.cos(angles), 1.0)
    sine = jnp.sin(angles)
    return cos_tab, jnp.where(first, -sine, 0.0), jnp.where(second, sine, 0.0)


def rotate(x, cos_tab, minus, plus):
    ahead = pltpu.roll(x, PAIR - ROT // 2, 1)
    behind = pltpu.roll(x, ROT // 2, 1)
    return x * cos_tab + ahead * minus + behind * plus


def head_lanes(x, head):
    lane = lax.broadcasted_iota(jnp.int32, x.shape, 1)
    return jnp.where((lane < HD) == (head == 0), x, jnp.zeros_like(x))


def transposed(x):
    return x.astype(jnp.float32).T.astype(x.dtype)


def causal_exp(scores, row_block, block):
    e = jnp.exp(scores)
    if row_block:
        done = e[: row_block * block]
    last = e[row_block * block :]
    key = lax.broadcasted_iota(jnp.int32, last.shape, 0)
    query = lax.broadcasted_iota(jnp.int32, last.shape, 1)
    last = jnp.where(key <= query, last, 0.0)
    return jnp.concatenate([done, last], axis=0) if row_block else last


def attend_kernel(block, mq, mk, mv, cos_ref, minus_ref, plus_ref, q_out, k_out, v_out, o_out):
    shape = q_out.shape
    length = shape[0] * shape[2]
    tabs = (cos_ref[...], minus_ref[...], plus_ref[...])
    q = rotate(mq[...].reshape(length, PAIR), *tabs).astype(jnp.bfloat16)
    k = rotate(mk[...].reshape(length, PAIR), *tabs).astype(jnp.bfloat16)
    v = mv[...].reshape(length, PAIR).astype(jnp.bfloat16)
    q_out[...] = q.reshape(shape)
    k_out[...] = k.reshape(shape)
    v_out[...] = v.reshape(shape)
    qs = q * jnp.bfloat16(HD**-0.5)
    vt = transposed(v)
    q_heads = [head_lanes(qs, h) for h in range(2)]
    rows = []
    for i in range(length // block):
        n = (i + 1) * block
        both = []
        for h in range(2):
            e = causal_exp(nt(k[:n], q_heads[h][i * block : n]), i, block)
            inv = 1.0 / jnp.sum(e, axis=0, keepdims=True)
            p = (e * inv).astype(jnp.bfloat16)
            both.append(nn(vt[h * HD : (h + 1) * HD, :n], p))
        rows.append(jnp.concatenate(both, axis=0).T)
    o_out[...] = jnp.concatenate(rows, axis=0).astype(jnp.bfloat16).reshape(shape)


def attend_back_kernel(block, q_ref, k_ref, v_ref, do_ref, cos_ref, minus_ref, plus_ref,
                       dq_out, dk_out, dv_out, dk_acc, dv_acc):
    shape = dq_out.shape
    length = shape[0] * shape[2]
    tabs = (cos_ref[...], -minus_ref[...], -plus_ref[...])
    scale = HD**-0.5
    q = q_ref[...].reshape(length, PAIR) * jnp.bfloat16(scale)
    k = k_ref[...].reshape(length, PAIR)
    v = v_ref[...].reshape(length, PAIR)
    do = do_ref[...].reshape(length, PAIR)
    kt = transposed(k)
    q_heads = [head_lanes(q, h) for h in range(2)]
    do_heads = [head_lanes(do, h) for h in range(2)]
    dk_acc[...] = jnp.zeros_like(dk_acc)
    dv_acc[...] = jnp.zeros_like(dv_acc)
    rows = []
    for i in range(length // block):
        n = (i + 1) * block
        both = []
        for h in range(2):
            q_i = q_heads[h][i * block : n]
            do_i = do_heads[h][i * block : n]
            e = causal_exp(nt(k[:n], q_i), i, block)
            p = e * (1.0 / jnp.sum(e, axis=0, keepdims=True))
            dp = nt(v[:n], do_i)
            inner = jnp.sum(p * dp, axis=0, keepdims=True)
            ds = (p * (dp - inner)).astype(jnp.bfloat16)
            dv_acc[:n] += nn(p.astype(jnp.bfloat16), do_i)
            dk_acc[:n] += nn(ds, q_i)
            both.append(nn(kt[h * HD : (h + 1) * HD, :n], ds))
        rows.append(jnp.concatenate(both, axis=0).T)

    def finish(g):
        return g.astype(jnp.bfloat16).astype(jnp.float32)

    dq = finish(jnp.concatenate(rows, axis=0) * scale)
    dq_out[...] = rotate(dq, *tabs).astype(jnp.bfloat16).reshape(shape)
    dk_out[...] = rotate(finish(dk_acc[...]), *tabs).astype(jnp.bfloat16).reshape(shape)
    dv_out[...] = dv_acc[...].astype(jnp.bfloat16).reshape(shape)


def attention_specs(parts, seqs, local_len, width):
    pairs = width // PAIR

    def spec(offset):
        return pl.BlockSpec((parts, 1, local_len, PAIR), lambda i, j: (0, i, 0, offset * pairs + j))

    length = parts * local_len
    tab = pl.BlockSpec((length, PAIR), lambda i, j: (0, 0))
    return spec, tab, (seqs, pairs), min(256, length)


def attend(m, tabs, width):
    parts, seqs, local_len, _ = m.shape
    spec, tab, grid, block = attention_specs(parts, seqs, local_len, width)
    out = jax.ShapeDtypeStruct((parts, seqs, local_len, width), jnp.bfloat16)
    work = seqs * (width // HD) * (parts * local_len) ** 2
    return pl.pallas_call(
        functools.partial(attend_kernel, block),
        grid=grid,
        in_specs=[spec(0), spec(1), spec(2), tab, tab, tab],
        out_specs=[spec(0)] * 4,
        out_shape=[out] * 4,
        compiler_params=pltpu.CompilerParams(vmem_limit_bytes=48 << 20),
        cost_estimate=pl.CostEstimate(
            flops=work * HD * 4, bytes_accessed=m.size * 4 + out.size * 8, transcendentals=work
        ),
        name="attend",
    )(m, m, m, *tabs)


def attend_back(q, k, v, do, tabs):
    parts, seqs, local_len, width = q.shape
    spec, tab, grid, block = attention_specs(parts, seqs, local_len, width)
    out = jax.ShapeDtypeStruct(q.shape, jnp.bfloat16)
    length = parts * local_len
    work = seqs * (width // HD) * length**2
    return pl.pallas_call(
        functools.partial(attend_back_kernel, block),
        grid=grid,
        in_specs=[spec(0)] * 4 + [tab] * 3,
        out_specs=[spec(0)] * 3,
        out_shape=[out] * 3,
        scratch_shapes=[pltpu.VMEM((length, PAIR), jnp.float32)] * 2,
        compiler_params=pltpu.CompilerParams(vmem_limit_bytes=48 << 20),
        cost_estimate=pl.CostEstimate(
            flops=work * HD * 10, bytes_accessed=out.size * 14, transcendentals=work
        ),
        name="attend_back",
    )(q, k, v, do, *tabs)


def mid_kernel(core_ref, o_ref, mine_ref, other_ref, x_ref, gain_ref, shift_ref, x1_out, a_out):
    step = pl.program_id(0)
    core = core_ref[0]

    @pl.when(step == 0)
    def _():
        x1_out[...] = x_ref[...].astype(jnp.float32)

    x1_out[...] += nn(o_ref[core], mine_ref[0]) + nn(o_ref[1 - core], other_ref[0])

    @pl.when(step == pl.num_programs(0) - 1)
    def _():
        xh, _ = norm_stats(x1_out[...])
        a_out[...] = (xh * gain_ref[...] + shift_ref[...]).astype(jnp.bfloat16)


def mid(core, o, mine, other, x, gain, shift):
    parts, rows, head_width = o.shape
    width = x.shape[1]
    whole = lambda shape: pl.BlockSpec(shape, lambda i, c: (0, 0))
    return pl.pallas_call(
        mid_kernel,
        grid_spec=pltpu.PrefetchScalarGridSpec(
            num_scalar_prefetch=1,
            grid=(parts // 2,),
            in_specs=[
                pl.BlockSpec((2, rows, head_width), lambda i, c: (i, 0, 0)),
                pl.BlockSpec((1, head_width, width), lambda i, c: (i, 0, 0)),
                pl.BlockSpec((1, head_width, width), lambda i, c: (i, 0, 0)),
                whole((rows, width)),
                whole((1, width)),
                whole((1, width)),
            ],
            out_specs=[whole((rows, width)), whole((rows, width))],
        ),
        out_shape=[
            jax.ShapeDtypeStruct((rows, width), jnp.float32),
            jax.ShapeDtypeStruct((rows, width), jnp.bfloat16),
        ],
        compiler_params=pltpu.CompilerParams(vmem_limit_bytes=48 << 20),
        cost_estimate=pl.CostEstimate(
            flops=2 * rows * width * width,
            bytes_accessed=2 * width * width + 10 * rows * width,
            transcendentals=0,
        ),
        name="mid",
    )(core, o, mine, other, x, gain[None, :], shift[None, :])


def mid_back_kernel(count, core_ref, *refs):
    pieces = refs[:count]
    x1_ref, dy_ref, gain_ref, mine_ref, other_ref = refs[count : count + 5]
    dx1_out, dxl_out, do_out, gain_out, shift_out = refs[count + 5 :]
    core = core_ref[0]

    @pl.when(pl.program_id(0) == 0)
    def _():
        dn = pieces[0][...].astype(jnp.float32)
        for piece in pieces[1:]:
            dn = dn + piece[...].astype(jnp.float32)
        xh, r = norm_stats(x1_ref[...])
        gain_out[...] = jnp.sum(dn * xh, axis=0, keepdims=True)
        shift_out[...] = jnp.sum(dn, axis=0, keepdims=True)
        dx1 = dy_ref[...].astype(jnp.float32) + norm_back(dn, xh, r, gain_ref[...])
        dx1_out[...] = dx1
        dxl_out[...] = dx1.astype(jnp.bfloat16)

    dxl = dxl_out[...]
    do_out[core] = nt(dxl, mine_ref[0]).astype(jnp.bfloat16)
    do_out[1 - core] = nt(dxl, other_ref[0]).astype(jnp.bfloat16)


def mid_back(core, pieces, x1, dy, gain, mine, other):
    rows, width = x1.shape
    halves, head_width, _ = mine.shape
    whole = lambda shape: pl.BlockSpec(shape, lambda i, c: (0, 0))
    full = whole((rows, width))
    weight = pl.BlockSpec((1, head_width, width), lambda i, c: (i, 0, 0))
    return pl.pallas_call(
        functools.partial(mid_back_kernel, len(pieces)),
        grid_spec=pltpu.PrefetchScalarGridSpec(
            num_scalar_prefetch=1,
            grid=(halves,),
            in_specs=[full] * (len(pieces) + 2) + [whole((1, width)), weight, weight],
            out_specs=[
                full,
                full,
                pl.BlockSpec((2, rows, head_width), lambda i, c: (i, 0, 0)),
                whole((1, width)),
                whole((1, width)),
            ],
        ),
        out_shape=[
            jax.ShapeDtypeStruct((rows, width), jnp.float32),
            jax.ShapeDtypeStruct((rows, width), jnp.bfloat16),
            jax.ShapeDtypeStruct((2 * halves, rows, head_width), jnp.bfloat16),
            jax.ShapeDtypeStruct((1, width), jnp.float32),
            jax.ShapeDtypeStruct((1, width), jnp.float32),
        ],
        compiler_params=pltpu.CompilerParams(vmem_limit_bytes=56 << 20),
        cost_estimate=pl.CostEstimate(
            flops=2 * rows * width * width,
            bytes_accessed=2 * width * width + 20 * rows * width,
            transcendentals=0,
        ),
        name="mid_back",
    )(core, *pieces, x1, dy, gain[None, :], mine, other)


def back_project_kernel(dm_ref, w_ref, side_ref, out_ref):
    width = w_ref.shape[0]
    out_ref[:, :width] = nt(dm_ref[...], w_ref[...]).astype(jnp.bfloat16)
    out_ref[:, width:] = side_ref[...]


def back_project(dm, w, side):
    rows, cols = dm.shape
    width = w.shape[0]
    extra = side.shape[1]
    block = min(256, rows)
    return pl.pallas_call(
        back_project_kernel,
        grid=(rows // block,),
        in_specs=[
            pl.BlockSpec((block, cols), lambda i: (i, 0)),
            pl.BlockSpec((width, cols), lambda i: (0, 0)),
            pl.BlockSpec((block, extra), lambda i: (i, 0)),
        ],
        out_specs=pl.BlockSpec((block, width + extra), lambda i: (i, 0)),
        out_shape=jax.ShapeDtypeStruct((rows, width + extra), jnp.bfloat16),
        compiler_params=pltpu.CompilerParams(vmem_limit_bytes=48 << 20),
        cost_estimate=pl.CostEstimate(
            flops=2 * rows * width * cols,
            bytes_accessed=2 * rows * (width + cols + 2 * extra) + 2 * width * cols,
            transcendentals=0,
        ),
        name="back_project",
    )(dm, w, side)


def third_rounds(parts):
    left = {s: [(j, (j * parts + s) // 3, (j * parts + s) % 3) for j in range(3)] for s in range(parts)}
    rounds = []
    for _ in range(3):
        owner = {}

        def place(s, seen):
            for edge in left[s]:
                d = edge[1]
                if d in seen:
                    continue
                seen.add(d)
                if d not in owner or place(owner[d][0], seen):
                    owner[d] = (s, edge)
                    return True
            return False

        for s in range(parts):
            place(s, set())
        send = [0] * parts
        slot = [0] * parts
        pairs = []
        for d, (s, edge) in owner.items():
            left[s].remove(edge)
            send[s] = edge[0]
            slot[d] = edge[2]
            pairs.append((s, d))
        rounds.append((sorted(pairs), send, slot))
    return rounds


def contiguous_thirds(block, parts, me):
    got = []
    slots = []
    for pairs, send, slot in third_rounds(parts):
        piece = lax.dynamic_index_in_dim(block, jnp.array(send)[me], 1, keepdims=False)
        got.append(lax.ppermute(piece, "seq", pairs))
        slots.append(jnp.array(slot)[me])
    out = []
    for k in range(3):
        out.append(jnp.where(slots[0] == k, got[0], jnp.where(slots[1] == k, got[1], got[2])))
    return jnp.concatenate(out, axis=1)


def after(x, *done):
    return lax.optimization_barrier((x, *done))[0]


def flip_pairs(parts, j):
    return [(i, i ^ j) for i in range(parts)]


def gather_flips(block, parts):
    return [block] + [lax.ppermute(block, "fsdp", flip_pairs(parts, j)) for j in range(1, parts)]


def send_flips(pieces, parts):
    return [pieces[0]] + [
        lax.ppermute(pieces[j], "fsdp", flip_pairs(parts, j)) for j in range(1, parts)
    ]


def total(pieces):
    out = pieces[0].astype(jnp.float32)
    for piece in pieces[1:]:
        out = out + piece.astype(jnp.float32)
    return out


def project_kernel(x_ref, gain_ref, shift_ref, w_ref, bias_ref, m_out, a_out):
    x = x_ref[...].astype(jnp.float32)
    xh, _ = norm_stats(x)
    a = (xh * gain_ref[...] + shift_ref[...]).astype(jnp.bfloat16)
    a_out[...] = a
    m_out[...] = nn(a, w_ref[...]) + bias_ref[...]


def project(x, gain, shift, w, bias):
    rows, width = x.shape
    cols = w.shape[1]
    block = min(256, rows)
    whole = lambda shape: pl.BlockSpec(shape, lambda i: (0, 0))
    return pl.pallas_call(
        project_kernel,
        grid=(rows // block,),
        in_specs=[
            pl.BlockSpec((block, width), lambda i: (i, 0)),
            whole((1, width)),
            whole((1, width)),
            whole((width, cols)),
            whole((1, cols)),
        ],
        out_specs=[
            pl.BlockSpec((block, cols), lambda i: (i, 0)),
            pl.BlockSpec((block, width), lambda i: (i, 0)),
        ],
        out_shape=[
            jax.ShapeDtypeStruct((rows, cols), jnp.float32),
            jax.ShapeDtypeStruct((rows, width), jnp.bfloat16),
        ],
        compiler_params=pltpu.CompilerParams(vmem_limit_bytes=48 << 20),
        cost_estimate=pl.CostEstimate(
            flops=2 * rows * width * cols,
            bytes_accessed=rows * width * 4 + rows * cols * 4 + width * cols * 2,
            transcendentals=0,
        ),
        name="project",
    )(x, gain[None, :], shift[None, :], w, bias[None, :])


def to_rows(block, fsdp_parts, here):
    rows = block.shape[2] // fsdp_parts
    pieces = []
    for j in range(fsdp_parts):
        piece = lax.dynamic_slice_in_dim(block, (here ^ j) * rows, rows, 2)
        pieces.append(lax.ppermute(piece, "fsdp", flip_pairs(fsdp_parts, j)) if j else piece)
    return pieces


def to_columns(blocks, seq_parts, me_seq):
    fsdp_parts = blocks.shape[0]
    ratio = seq_parts // fsdp_parts
    out = jnp.zeros_like(blocks)
    for r in range(fsdp_parts):
        pairs = [
            (s, ratio * (s % fsdp_parts ^ r) + s // fsdp_parts) for s in range(seq_parts)
        ]
        piece = lax.dynamic_index_in_dim(blocks, me_seq % fsdp_parts ^ r, 0, keepdims=False)
        got = lax.ppermute(piece, "seq", pairs)
        out = lax.dynamic_update_index_in_dim(out, got, me_seq // ratio ^ r, 0)
    _, count, part, rows = blocks.shape
    return out.transpose(1, 0, 2, 3).reshape(count, fsdp_parts * part, rows)


def on_device(
    tokens,
    attn_gain,
    attn_shift,
    qkv_weight,
    qkv_bias,
    out_weight,
    ffn_gain,
    ffn_shift,
    gate_weight,
    up_weight,
    down_weight,
    cotangent,
):
    f32, bf16 = jnp.float32, jnp.bfloat16
    seqs, local_len, width = tokens.shape
    S = lax.axis_size("seq")
    F = lax.axis_size("fsdp")
    me = lax.axis_index("seq")
    devices = S * F
    rows = seqs * local_len
    all_rows = S * rows
    head_width = width // S
    ff_rows, _ = down_weight.shape
    shard = width // F

    ratio = S // F
    if ratio != 2 or F & (F - 1):
        raise ValueError("unsupported mesh")
    even = me % 2 == 0
    core = (me % 2).reshape(1).astype(jnp.int32)
    mate = flip_pairs(S, 1)
    here = lax.axis_index("fsdp")

    def natural(pieces):
        out = jnp.zeros((F, *pieces[0].shape), pieces[0].dtype)
        for j, piece in enumerate(pieces):
            out = lax.dynamic_update_index_in_dim(out, piece, here ^ j, 0)
        return out

    x_all = lax.all_gather(tokens, "seq", axis=0).reshape(all_rows, width)
    small = jnp.concatenate([attn_gain, attn_shift, ffn_gain, ffn_shift, qkv_bias])
    small = natural(gather_flips(small, F))
    params = [small[:, i * shard : (i + 1) * shard].reshape(width).astype(f32) for i in range(4)]
    gain1, shift1, gain2, shift2 = params
    bias = small[:, 4 * shard :].reshape(3, S, head_width).astype(f32)
    bias = lax.dynamic_index_in_dim(bias, me, 1, keepdims=False).reshape(3 * head_width)
    qkv_part = jnp.concatenate(
        [
            lax.dynamic_slice_in_dim(qkv_weight, j * width + me * head_width, head_width, 1)
            for j in range(3)
        ],
        axis=1,
    )
    w_qkv = natural(gather_flips(qkv_part, F)).reshape(width, 3 * head_width)

    fetched = jnp.stack(
        [
            jnp.where(
                even,
                gate_weight[:, f * ff_rows : (f + 1) * ff_rows],
                up_weight[:, f * ff_rows : (f + 1) * ff_rows],
            )
            for f in range(F)
        ]
    )
    fetched = after(fetched, qkv_part)
    w_mine = lax.all_to_all(fetched, "fsdp", split_axis=0, concat_axis=0, tiled=True)
    w_mine = w_mine.reshape(width, ff_rows)
    w_other = lax.ppermute(w_mine, "seq", mate)
    out_half = lax.dynamic_slice_in_dim(out_weight, me % 2 * head_width, head_width, 0)
    out_mine = lax.all_gather(out_half, "fsdp", axis=0)

    tabs = rotary_tables(S * local_len)
    m, a1 = project(x_all, gain1, shift1, w_qkv, bias)
    q, k, v, o = attend(m.reshape(S, seqs, local_len, 3 * head_width), tabs, head_width)
    o_got = lax.all_to_all(o, "seq", split_axis=0, concat_axis=0, tiled=True)
    out_other = lax.ppermute(out_mine, "seq", mate)
    dy_own = cotangent.reshape(rows, width)
    dy_early = after(dy_own, o)
    dy_pieces = [dy_own]
    for j in range(1, F - 1):
        dy_pieces.append(lax.ppermute(dy_early, "fsdp", flip_pairs(F, j)))
    o_got = o_got.reshape(S, rows, head_width)

    x_own = tokens.reshape(rows, width)
    x1, a2 = mid(core, o_got, out_mine, out_other, x_own, gain2, shift2)
    a2_all = lax.all_gather(a2, "fsdp", axis=0, tiled=True)
    dy_pieces.append(lax.ppermute(after(dy_own, a2_all), "fsdp", flip_pairs(F, F - 1)))
    dy_all = natural(dy_pieces).reshape(F * rows, width)

    first = nn(a2_all, w_mine)
    second = nn(a2_all, w_other)
    g = jnp.where(even, first, second)
    u = jnp.where(even, second, first)
    sig = jax.nn.sigmoid(g)
    silu = g * sig
    hid = (silu * u).astype(bf16)
    down_grad_part = tn(dy_all, hid).astype(bf16)
    down_grad = lax.psum_scatter(down_grad_part, "seq", scatter_dimension=0, tiled=True)
    dh = nt(after(dy_all, down_grad_part), down_weight)
    dg = (dh * u * sig * (1.0 + g * (1.0 - sig))).astype(bf16)
    du = (dh * silu).astype(bf16)
    d_first = jnp.where(even, dg, du)
    d_second = jnp.where(even, du, dg)
    dn2_part = (nt(d_first, w_mine) + nt(d_second, w_other)).astype(bf16)
    dn2_part = dn2_part.reshape(F, rows, width)
    dn2_pieces = []
    for j in range(F):
        dn2_pieces.append(lax.dynamic_index_in_dim(dn2_part, here ^ j, 0, keepdims=False))
    dgu = after(jnp.concatenate([dg, du], axis=1), dn2_pieces)
    for j in range(1, F):
        dn2_pieces[j] = lax.ppermute(dn2_pieces[j], "fsdp", flip_pairs(F, j))
    both_part = tn(dgu, a2_all).astype(bf16).reshape(2, ff_rows, width)
    both = lax.psum_scatter(both_part, "seq", scatter_dimension=1, tiled=True)
    hid_late = after(hid, both_part)
    down_part = nn(hid_late, down_weight).astype(bf16)

    dn2_pieces = after(dn2_pieces, down_part)
    dx1, dxl, do_two, gain2_part, shift2_part = mid_back(
        core, dn2_pieces, x1, dy_own, gain2, out_mine, out_other
    )
    do = lax.all_to_all(do_two, "seq", split_axis=0, concat_axis=0, tiled=True)
    do = do.reshape(S, seqs, local_len, head_width)

    dxl_all = natural(gather_flips(dxl, F)).reshape(F * rows, width)
    o_got = after(o_got, dxl)
    o_pieces = []
    for j in range(F):
        piece = lax.dynamic_slice_in_dim(o_got, 2 * (here ^ j), 2, 0)
        o_pieces.append(lax.ppermute(piece, "fsdp", flip_pairs(F, j)) if j else piece)
    o_cols = natural(o_pieces).transpose(1, 0, 2, 3).reshape(2, F * rows, head_width)
    out_part = jnp.concatenate([tn(dxl_all, o_cols[h]) for h in range(2)], axis=1).astype(bf16)

    dq, dk, dv = attend_back(q, k, v, do, tabs)
    dm = jnp.concatenate([dq, dk, dv], axis=-1).reshape(all_rows, 3 * head_width)
    down_part = after(down_part, dm).reshape(F, rows, width)
    down_pieces = send_flips(
        [lax.dynamic_index_in_dim(down_part, here ^ j, 0, keepdims=False) for j in range(F)], F
    )
    joint_part = back_project(dm, w_qkv, out_part)
    joint = lax.psum_scatter(joint_part, "seq", scatter_dimension=0, tiled=True)
    dn1 = joint[:, :width].astype(f32)
    out_result = joint[:, width:].T.astype(f32)
    a1_late, both = after((a1, both), joint_part)
    both_pieces = to_rows(both, F, here)
    qkv_part_grad = tn(a1_late, dm).astype(bf16)
    qkv_part_grad = qkv_part_grad.reshape(F, shard, 3 * head_width)
    qkv_pieces = [
        lax.dynamic_index_in_dim(qkv_part_grad, here ^ j, 0, keepdims=False) for j in range(F)
    ]
    dm, dn1_late, x_late, down_grad, both_pieces, down_pieces = after(
        (dm, joint_part, x_all, down_grad, both_pieces, down_pieces), qkv_pieces
    )
    qkv_got = send_flips(qkv_pieces, F)
    qkv_sum = total(qkv_got).astype(bf16)
    qkv_result = contiguous_thirds(qkv_sum.reshape(shard, 3, head_width), S, me).astype(f32)
    both = to_columns(natural(both_pieces), S, me).astype(f32)
    gate_result, up_result = both[0].T, both[1].T
    layer_out = (x1 + total(down_pieces)).astype(bf16).reshape(tokens.shape)
    down_result = down_grad.T.astype(f32)

    bias_part = jnp.sum(dm, axis=0, dtype=f32).reshape(3, 1, head_width)
    bias_full = lax.dynamic_update_slice_in_dim(
        jnp.zeros((3, S, head_width), f32), bias_part, me, 1
    ).reshape(3 * width)
    xh_all, _ = norm_stats(x_late.astype(f32))
    dn1_late = dn1_late[:, :width].astype(f32)
    attn_gain_part = jnp.sum(dn1_late * xh_all, axis=0)
    attn_shift_part = jnp.sum(dn1_late, axis=0)
    small_parts = [
        attn_gain_part,
        attn_shift_part,
        bias_full[: 2 * width],
        bias_full[2 * width :],
        gain2_part[0],
        shift2_part[0],
    ]
    packed = jnp.concatenate([p.reshape(devices, -1) for p in small_parts], axis=1)
    packed = lax.all_to_all(packed, MESH_AXES, split_axis=0, concat_axis=0, tiled=True)
    packed = jnp.sum(packed, axis=0)
    results = []
    start = 0
    for p in small_parts:
        size = p.shape[0] // devices
        results.append(packed[start : start + size])
        start += size
    gain1_result, shift1_result, bias_result, value_result, gain2_result, shift2_result = results

    xh, r = norm_stats(x_own.astype(f32))
    tokens_grad = (dx1 + norm_back(dn1, xh, r, gain1)).reshape(tokens.shape)
    return (
        layer_out,
        tokens_grad,
        gain1_result,
        shift1_result,
        qkv_result,
        bias_result,
        value_result,
        out_result,
        gain2_result,
        shift2_result,
        gate_result,
        up_result,
        down_result,
    )


def solution(mesh):
    return jax.shard_map(
        on_device,
        mesh=mesh,
        in_specs=(
            P("fsdp", "seq", None),
            P("fsdp"),
            P("fsdp"),
            P("fsdp", None),
            P("fsdp"),
            P("fsdp", None),
            P("fsdp"),
            P("fsdp"),
            P("fsdp", None),
            P("fsdp", None),
            P("fsdp", None),
            P("fsdp", "seq", None),
        ),
        out_specs=(
            P("fsdp", "seq", None),
            P("fsdp", "seq", None),
            P(("seq", "fsdp")),
            P(("seq", "fsdp")),
            P("fsdp", "seq"),
            P(("seq", "fsdp")),
            P(("seq", "fsdp")),
            P("fsdp", "seq"),
            P(("seq", "fsdp")),
            P(("seq", "fsdp")),
            P("fsdp", "seq"),
            P("fsdp", "seq"),
            P("fsdp", "seq"),
        ),
        check_vma=False,
    )
```

```python
import functools

import jax
import jax.numpy as jnp
from jax import lax
from jax.experimental import pallas as pl
from jax.experimental.pallas import tpu as pltpu
from jax.sharding import PartitionSpec as P


HD = 64
ROT = 16
PAIR = 2 * HD
MESH_AXES = ("seq", "fsdp")


def nn(a, b):
    return lax.dot_general(a, b, (((1,), (0,)), ((), ())), preferred_element_type=jnp.float32)


def nt(a, b):
    return lax.dot_general(a, b, (((1,), (1,)), ((), ())), preferred_element_type=jnp.float32)


def tn(a, b):
    return lax.dot_general(a, b, (((0,), (0,)), ((), ())), preferred_element_type=jnp.float32)


def norm_stats(x):
    mean = jnp.mean(x, axis=-1, keepdims=True)
    center = x - mean
    var = jnp.mean(center * center, axis=-1, keepdims=True)
    r = lax.rsqrt(var + 1e-05)
    return center * r, r


def norm_back(dn, xh, r, gain):
    e = dn * gain
    return r * (
        e
        - jnp.mean(e, axis=-1, keepdims=True)
        - xh * jnp.mean(e * xh, axis=-1, keepdims=True)
    )


def rotary_tables(length):
    lane = jnp.arange(PAIR) % HD
    ladder = 10000.0 ** (-jnp.arange(0, ROT, 2, dtype=jnp.float32) / ROT)
    places = jnp.arange(length, dtype=jnp.float32)
    angles = places[:, None] * jnp.tile(ladder, PAIR // (ROT // 2))[None, :]
    first = (lane < ROT // 2)[None, :]
    second = ((lane >= ROT // 2) & (lane < ROT))[None, :]
    cos_tab = jnp.where(first | second, jnp.cos(angles), 1.0)
    sine = jnp.sin(angles)
    return cos_tab, jnp.where(first, -sine, 0.0), jnp.where(second, sine, 0.0)


def rotate(x, cos_tab, minus, plus):
    ahead = pltpu.roll(x, PAIR - ROT // 2, 1)
    behind = pltpu.roll(x, ROT // 2, 1)
    return x * cos_tab + ahead * minus + behind * plus


def head_lanes(x, head):
    lane = lax.broadcasted_iota(jnp.int32, x.shape, 1)
    return jnp.where((lane < HD) == (head == 0), x, jnp.zeros_like(x))


def transposed(x):
    return x.astype(jnp.float32).T.astype(x.dtype)


def causal_exp(scores, row_block, block):
    e = jnp.exp(scores)
    if row_block:
        done = e[: row_block * block]
    last = e[row_block * block :]
    key = lax.broadcasted_iota(jnp.int32, last.shape, 0)
    query = lax.broadcasted_iota(jnp.int32, last.shape, 1)
    last = jnp.where(key <= query, last, 0.0)
    return jnp.concatenate([done, last], axis=0) if row_block else last


def attend_kernel(block, mq, mk, mv, cos_ref, minus_ref, plus_ref, q_out, k_out, v_out, o_out):
    shape = q_out.shape
    length = shape[0] * shape[2]
    tabs = (cos_ref[...], minus_ref[...], plus_ref[...])
    q = rotate(mq[...].reshape(length, PAIR), *tabs).astype(jnp.bfloat16)
    k = rotate(mk[...].reshape(length, PAIR), *tabs).astype(jnp.bfloat16)
    v = mv[...].reshape(length, PAIR).astype(jnp.bfloat16)
    q_out[...] = q.reshape(shape)
    k_out[...] = k.reshape(shape)
    v_out[...] = v.reshape(shape)
    qs = q * jnp.bfloat16(HD**-0.5)
    vt = transposed(v)
    q_heads = [head_lanes(qs, h) for h in range(2)]
    rows = []
    for i in range(length // block):
        n = (i + 1) * block
        both = []
        for h in range(2):
            e = causal_exp(nt(k[:n], q_heads[h][i * block : n]), i, block)
            inv = 1.0 / jnp.sum(e, axis=0, keepdims=True)
            p = (e * inv).astype(jnp.bfloat16)
            both.append(nn(vt[h * HD : (h + 1) * HD, :n], p))
        rows.append(jnp.concatenate(both, axis=0).T)
    o_out[...] = jnp.concatenate(rows, axis=0).astype(jnp.bfloat16).reshape(shape)


def attend_back_kernel(block, q_ref, k_ref, v_ref, do_ref, cos_ref, minus_ref, plus_ref,
                       dq_out, dk_out, dv_out, dk_acc, dv_acc):
    shape = dq_out.shape
    length = shape[0] * shape[2]
    tabs = (cos_ref[...], -minus_ref[...], -plus_ref[...])
    scale = HD**-0.5
    q = q_ref[...].reshape(length, PAIR) * jnp.bfloat16(scale)
    k = k_ref[...].reshape(length, PAIR)
    v = v_ref[...].reshape(length, PAIR)
    do = do_ref[...].reshape(length, PAIR)
    kt = transposed(k)
    q_heads = [head_lanes(q, h) for h in range(2)]
    do_heads = [head_lanes(do, h) for h in range(2)]
    dk_acc[...] = jnp.zeros_like(dk_acc)
    dv_acc[...] = jnp.zeros_like(dv_acc)
    rows = []
    for i in range(length // block):
        n = (i + 1) * block
        both = []
        for h in range(2):
            q_i = q_heads[h][i * block : n]
            do_i = do_heads[h][i * block : n]
            e = causal_exp(nt(k[:n], q_i), i, block)
            p = e * (1.0 / jnp.sum(e, axis=0, keepdims=True))
            dp = nt(v[:n], do_i)
            inner = jnp.sum(p * dp, axis=0, keepdims=True)
            ds = (p * (dp - inner)).astype(jnp.bfloat16)
            dv_acc[:n] += nn(p.astype(jnp.bfloat16), do_i)
            dk_acc[:n] += nn(ds, q_i)
            both.append(nn(kt[h * HD : (h + 1) * HD, :n], ds))
        rows.append(jnp.concatenate(both, axis=0).T)

    def finish(g):
        return g.astype(jnp.bfloat16).astype(jnp.float32)

    dq = finish(jnp.concatenate(rows, axis=0) * scale)
    dq_out[...] = rotate(dq, *tabs).astype(jnp.bfloat16).reshape(shape)
    dk_out[...] = rotate(finish(dk_acc[...]), *tabs).astype(jnp.bfloat16).reshape(shape)
    dv_out[...] = dv_acc[...].astype(jnp.bfloat16).reshape(shape)


def attention_specs(parts, seqs, local_len, width):
    pairs = width // PAIR

    def spec(offset):
        return pl.BlockSpec((parts, 1, local_len, PAIR), lambda i, j: (0, i, 0, offset * pairs + j))

    length = parts * local_len
    tab = pl.BlockSpec((length, PAIR), lambda i, j: (0, 0))
    return spec, tab, (seqs, pairs), min(256, length)


def attend(m, tabs, width):
    parts, seqs, local_len, _ = m.shape
    spec, tab, grid, block = attention_specs(parts, seqs, local_len, width)
    out = jax.ShapeDtypeStruct((parts, seqs, local_len, width), jnp.bfloat16)
    work = seqs * (width // HD) * (parts * local_len) ** 2
    return pl.pallas_call(
        functools.partial(attend_kernel, block),
        grid=grid,
        in_specs=[spec(0), spec(1), spec(2), tab, tab, tab],
        out_specs=[spec(0)] * 4,
        out_shape=[out] * 4,
        compiler_params=pltpu.CompilerParams(vmem_limit_bytes=48 << 20),
        cost_estimate=pl.CostEstimate(
            flops=work * HD * 4, bytes_accessed=m.size * 4 + out.size * 8, transcendentals=work
        ),
        name="attend",
    )(m, m, m, *tabs)


def attend_back(q, k, v, do, tabs):
    parts, seqs, local_len, width = q.shape
    spec, tab, grid, block = attention_specs(parts, seqs, local_len, width)
    out = jax.ShapeDtypeStruct(q.shape, jnp.bfloat16)
    length = parts * local_len
    work = seqs * (width // HD) * length**2
    return pl.pallas_call(
        functools.partial(attend_back_kernel, block),
        grid=grid,
        in_specs=[spec(0)] * 4 + [tab] * 3,
        out_specs=[spec(0)] * 3,
        out_shape=[out] * 3,
        scratch_shapes=[pltpu.VMEM((length, PAIR), jnp.float32)] * 2,
        compiler_params=pltpu.CompilerParams(vmem_limit_bytes=48 << 20),
        cost_estimate=pl.CostEstimate(
            flops=work * HD * 10, bytes_accessed=out.size * 14, transcendentals=work
        ),
        name="attend_back",
    )(q, k, v, do, *tabs)


def mid_kernel(core_ref, o_ref, mine_ref, other_ref, x_ref, gain_ref, shift_ref, x1_out, a_out):
    step = pl.program_id(0)
    core = core_ref[0]

    @pl.when(step == 0)
    def _():
        x1_out[...] = x_ref[...].astype(jnp.float32)

    x1_out[...] += nn(o_ref[core], mine_ref[0]) + nn(o_ref[1 - core], other_ref[0])

    @pl.when(step == pl.num_programs(0) - 1)
    def _():
        xh, _ = norm_stats(x1_out[...])
        a_out[...] = (xh * gain_ref[...] + shift_ref[...]).astype(jnp.bfloat16)


def mid(core, o, mine, other, x, gain, shift):
    parts, rows, head_width = o.shape
    width = x.shape[1]
    whole = lambda shape: pl.BlockSpec(shape, lambda i, c: (0, 0))
    return pl.pallas_call(
        mid_kernel,
        grid_spec=pltpu.PrefetchScalarGridSpec(
            num_scalar_prefetch=1,
            grid=(parts // 2,),
            in_specs=[
                pl.BlockSpec((2, rows, head_width), lambda i, c: (i, 0, 0)),
                pl.BlockSpec((1, head_width, width), lambda i, c: (i, 0, 0)),
                pl.BlockSpec((1, head_width, width), lambda i, c: (i, 0, 0)),
                whole((rows, width)),
                whole((1, width)),
                whole((1, width)),
            ],
            out_specs=[whole((rows, width)), whole((rows, width))],
        ),
        out_shape=[
            jax.ShapeDtypeStruct((rows, width), jnp.float32),
            jax.ShapeDtypeStruct((rows, width), jnp.bfloat16),
        ],
        compiler_params=pltpu.CompilerParams(vmem_limit_bytes=48 << 20),
        cost_estimate=pl.CostEstimate(
            flops=2 * rows * width * width,
            bytes_accessed=2 * width * width + 10 * rows * width,
            transcendentals=0,
        ),
        name="mid",
    )(core, o, mine, other, x, gain[None, :], shift[None, :])


def mid_back_kernel(count, core_ref, *refs):
    pieces = refs[:count]
    x1_ref, dy_ref, gain_ref, mine_ref, other_ref = refs[count : count + 5]
    dx1_out, dxl_out, do_out, gain_out, shift_out = refs[count + 5 :]
    core = core_ref[0]

    @pl.when(pl.program_id(0) == 0)
    def _():
        dn = pieces[0][...].astype(jnp.float32)
        for piece in pieces[1:]:
            dn = dn + piece[...].astype(jnp.float32)
        xh, r = norm_stats(x1_ref[...])
        gain_out[...] = jnp.sum(dn * xh, axis=0, keepdims=True)
        shift_out[...] = jnp.sum(dn, axis=0, keepdims=True)
        dx1 = dy_ref[...].astype(jnp.float32) + norm_back(dn, xh, r, gain_ref[...])
        dx1_out[...] = dx1
        dxl_out[...] = dx1.astype(jnp.bfloat16)

    dxl = dxl_out[...]
    do_out[core] = nt(dxl, mine_ref[0]).astype(jnp.bfloat16)
    do_out[1 - core] = nt(dxl, other_ref[0]).astype(jnp.bfloat16)


def mid_back(core, pieces, x1, dy, gain, mine, other):
    rows, width = x1.shape
    halves, head_width, _ = mine.shape
    whole = lambda shape: pl.BlockSpec(shape, lambda i, c: (0, 0))
    full = whole((rows, width))
    weight = pl.BlockSpec((1, head_width, width), lambda i, c: (i, 0, 0))
    return pl.pallas_call(
        functools.partial(mid_back_kernel, len(pieces)),
        grid_spec=pltpu.PrefetchScalarGridSpec(
            num_scalar_prefetch=1,
            grid=(halves,),
            in_specs=[full] * (len(pieces) + 2) + [whole((1, width)), weight, weight],
            out_specs=[
                full,
                full,
                pl.BlockSpec((2, rows, head_width), lambda i, c: (i, 0, 0)),
                whole((1, width)),
                whole((1, width)),
            ],
        ),
        out_shape=[
            jax.ShapeDtypeStruct((rows, width), jnp.float32),
            jax.ShapeDtypeStruct((rows, width), jnp.bfloat16),
            jax.ShapeDtypeStruct((2 * halves, rows, head_width), jnp.bfloat16),
            jax.ShapeDtypeStruct((1, width), jnp.float32),
            jax.ShapeDtypeStruct((1, width), jnp.float32),
        ],
        compiler_params=pltpu.CompilerParams(vmem_limit_bytes=56 << 20),
        cost_estimate=pl.CostEstimate(
            flops=2 * rows * width * width,
            bytes_accessed=2 * width * width + 20 * rows * width,
            transcendentals=0,
        ),
        name="mid_back",
    )(core, *pieces, x1, dy, gain[None, :], mine, other)


def joint_kernel(count, *refs):
    dq_ref, dk_ref, dv_ref, w_ref = refs[:4]
    x_refs = refs[4 : 4 + count]
    o_refs = refs[4 + count : 4 + 2 * count]
    out_ref = refs[-1]
    width, cols = w_ref.shape
    part = cols // 3
    w = w_ref[...]
    total = nt(dq_ref[...], w[:, :part])
    total = total + nt(dk_ref[...], w[:, part : 2 * part])
    total = total + nt(dv_ref[...], w[:, 2 * part :])
    out_ref[:, :width] = total.astype(jnp.bfloat16)
    for h in range(2):
        side = tn(x_refs[0][...], o_refs[0][h])
        for x_ref, o_ref in zip(x_refs[1:], o_refs[1:]):
            side = side + tn(x_ref[...], o_ref[h])
        start = width + h * part
        out_ref[:, start : start + part] = side.astype(jnp.bfloat16)


def joint(dq, dk, dv, w, xs, os):
    all_rows, part = dq.shape
    width, cols = w.shape
    rows = xs[0].shape[0]
    count = len(xs)
    parts = width // part
    block = all_rows // parts
    if block != part:
        raise ValueError("unsupported shape")
    row_block = pl.BlockSpec((block, part), lambda i: (i, 0))
    return pl.pallas_call(
        functools.partial(joint_kernel, count),
        grid=(parts,),
        in_specs=[row_block] * 3
        + [pl.BlockSpec((width, cols), lambda i: (0, 0))]
        + [pl.BlockSpec((rows, part), lambda i: (0, i))] * count
        + [pl.BlockSpec((2, rows, part), lambda i: (0, 0, 0))] * count,
        out_specs=pl.BlockSpec((block, width + 2 * part), lambda i: (i, 0)),
        out_shape=jax.ShapeDtypeStruct((all_rows, width + 2 * part), jnp.bfloat16),
        compiler_params=pltpu.CompilerParams(vmem_limit_bytes=48 << 20),
        cost_estimate=pl.CostEstimate(
            flops=2 * all_rows * width * cols + 4 * count * rows * width * part,
            bytes_accessed=4 * all_rows * (width + cols) + 2 * width * cols,
            transcendentals=0,
        ),
        name="joint",
    )(dq, dk, dv, w, *xs, *os)


def pick_kernel(counts, core_ref, gate_ref, up_ref, out_ref):
    blocks, fsdp_parts, part = counts

    def pick(source):
        rows = source[...]
        for f in range(fsdp_parts):
            starts = [(t * fsdp_parts + f) * part for t in range(blocks)]
            out_ref[f] = jnp.concatenate([rows[:, a : a + part] for a in starts], axis=1)

    @pl.when(core_ref[0] == 0)
    def _():
        pick(gate_ref)

    @pl.when(core_ref[0] != 0)
    def _():
        pick(up_ref)


def pick(core, gate, up, blocks, fsdp_parts):
    rows, cols = gate.shape
    part = cols // (blocks * fsdp_parts)
    block = min(64, rows)
    return pl.pallas_call(
        functools.partial(pick_kernel, (blocks, fsdp_parts, part)),
        grid_spec=pltpu.PrefetchScalarGridSpec(
            num_scalar_prefetch=1,
            grid=(rows // block,),
            in_specs=[
                pl.BlockSpec((block, cols), lambda i, c: (jnp.where(c[0] == 0, i, 0), 0)),
                pl.BlockSpec((block, cols), lambda i, c: (jnp.where(c[0] == 0, 0, i), 0)),
            ],
            out_specs=pl.BlockSpec((fsdp_parts, block, blocks * part), lambda i, c: (0, i, 0)),
        ),
        out_shape=jax.ShapeDtypeStruct((fsdp_parts, rows, blocks * part), gate.dtype),
        compiler_params=pltpu.CompilerParams(vmem_limit_bytes=32 << 20),
        cost_estimate=pl.CostEstimate(flops=0, bytes_accessed=4 * rows * cols, transcendentals=0),
        name="pick",
    )(core, gate, up)


def third_rounds(parts):
    left = {s: [(j, (j * parts + s) // 3, (j * parts + s) % 3) for j in range(3)] for s in range(parts)}
    rounds = []
    for _ in range(3):
        owner = {}

        def place(s, seen):
            for edge in left[s]:
                d = edge[1]
                if d in seen:
                    continue
                seen.add(d)
                if d not in owner or place(owner[d][0], seen):
                    owner[d] = (s, edge)
                    return True
            return False

        for s in range(parts):
            place(s, set())
        send = [0] * parts
        slot = [0] * parts
        pairs = []
        for d, (s, edge) in owner.items():
            left[s].remove(edge)
            send[s] = edge[0]
            slot[d] = edge[2]
            pairs.append((s, d))
        rounds.append((sorted(pairs), send, slot))
    return rounds


def contiguous_thirds(block, parts, me):
    got = []
    slots = []
    for pairs, send, slot in third_rounds(parts):
        piece = lax.dynamic_index_in_dim(block, jnp.array(send)[me], 1, keepdims=False)
        got.append(lax.ppermute(piece, "seq", pairs))
        slots.append(jnp.array(slot)[me])
    out = []
    for k in range(3):
        out.append(jnp.where(slots[0] == k, got[0], jnp.where(slots[1] == k, got[1], got[2])))
    return jnp.concatenate(out, axis=1)


def after(x, *done):
    return lax.optimization_barrier((x, *done))[0]


def flip_pairs(parts, j):
    return [(i, i ^ j) for i in range(parts)]


def gather_flips(block, parts):
    return [block] + [lax.ppermute(block, "fsdp", flip_pairs(parts, j)) for j in range(1, parts)]


def relay_near(block, parts):
    if parts != 4:
        return gather_flips(block, parts)[1:]
    return [lax.ppermute(block, "fsdp", flip_pairs(parts, j)) for j in (1, 2)]


def relay_far(block, near, parts):
    if parts != 4:
        return [block, *near]
    one, two = near
    half = block.shape[0] // 2
    head = lax.ppermute(two[:half], "fsdp", flip_pairs(parts, 1))
    tail = lax.ppermute(one[half:], "fsdp", flip_pairs(parts, 2))
    return [block, one, two, (head, tail)]


def send_flips(pieces, parts):
    return [pieces[0]] + [
        lax.ppermute(pieces[j], "fsdp", flip_pairs(parts, j)) for j in range(1, parts)
    ]


def total(pieces):
    out = pieces[0].astype(jnp.float32)
    for piece in pieces[1:]:
        out = out + piece.astype(jnp.float32)
    return out


def project_kernel(x_ref, gain_ref, shift_ref, w_ref, bias_ref, m_out, a_out):
    x = x_ref[...].astype(jnp.float32)
    xh, _ = norm_stats(x)
    a = (xh * gain_ref[...] + shift_ref[...]).astype(jnp.bfloat16)
    a_out[...] = a
    m_out[...] = nn(a, w_ref[...]) + bias_ref[...]


def project(x, gain, shift, w, bias):
    rows, width = x.shape
    cols = w.shape[1]
    block = min(256, rows)
    whole = lambda shape: pl.BlockSpec(shape, lambda i: (0, 0))
    return pl.pallas_call(
        project_kernel,
        grid=(rows // block,),
        in_specs=[
            pl.BlockSpec((block, width), lambda i: (i, 0)),
            whole((1, width)),
            whole((1, width)),
            whole((width, cols)),
            whole((1, cols)),
        ],
        out_specs=[
            pl.BlockSpec((block, cols), lambda i: (i, 0)),
            pl.BlockSpec((block, width), lambda i: (i, 0)),
        ],
        out_shape=[
            jax.ShapeDtypeStruct((rows, cols), jnp.float32),
            jax.ShapeDtypeStruct((rows, width), jnp.bfloat16),
        ],
        compiler_params=pltpu.CompilerParams(vmem_limit_bytes=48 << 20),
        cost_estimate=pl.CostEstimate(
            flops=2 * rows * width * cols,
            bytes_accessed=rows * width * 4 + rows * cols * 4 + width * cols * 2,
            transcendentals=0,
        ),
        name="project",
    )(x, gain[None, :], shift[None, :], w, bias[None, :])


def to_rows(block, fsdp_parts, here):
    rows = block.shape[2] // fsdp_parts
    pieces = []
    for j in range(fsdp_parts):
        piece = lax.dynamic_slice_in_dim(block, (here ^ j) * rows, rows, 2)
        pieces.append(lax.ppermute(piece, "fsdp", flip_pairs(fsdp_parts, j)) if j else piece)
    return pieces


def on_device(
    tokens,
    attn_gain,
    attn_shift,
    qkv_weight,
    qkv_bias,
    out_weight,
    ffn_gain,
    ffn_shift,
    gate_weight,
    up_weight,
    down_weight,
    cotangent,
):
    f32, bf16 = jnp.float32, jnp.bfloat16
    seqs, local_len, width = tokens.shape
    S = lax.axis_size("seq")
    F = lax.axis_size("fsdp")
    me = lax.axis_index("seq")
    devices = S * F
    rows = seqs * local_len
    all_rows = S * rows
    head_width = width // S
    ff_rows, _ = down_weight.shape
    shard = width // F

    ratio = S // F
    if ratio != 2 or F & (F - 1):
        raise ValueError("unsupported mesh")
    ff_block = F * ff_rows // S
    ff_part = ff_block // F
    even = me % 2 == 0
    core = (me % 2).reshape(1).astype(jnp.int32)
    mate = flip_pairs(S, 1)
    here = lax.axis_index("fsdp")

    def natural(pieces):
        out = jnp.zeros((F, *pieces[0].shape), pieces[0].dtype)
        rest = (0,) * (pieces[0].ndim - 1)
        for j, piece in enumerate(pieces):
            start = 0
            for part in piece if isinstance(piece, tuple) else (piece,):
                out = lax.dynamic_update_slice(out, part[None], (here ^ j, start, *rest))
                start += part.shape[0]
        return out

    x_all = lax.all_gather(tokens, "seq", axis=0).reshape(all_rows, width)
    small = jnp.concatenate([attn_gain, attn_shift, ffn_gain, ffn_shift, qkv_bias])
    small = natural(gather_flips(small, F))
    params = [small[:, i * shard : (i + 1) * shard].reshape(width).astype(f32) for i in range(4)]
    gain1, shift1, gain2, shift2 = params
    bias = small[:, 4 * shard :].reshape(3, S, head_width).astype(f32)
    bias = lax.dynamic_index_in_dim(bias, me, 1, keepdims=False).reshape(3 * head_width)
    qkv_part = jnp.concatenate(
        [
            lax.dynamic_slice_in_dim(qkv_weight, j * width + me * head_width, head_width, 1)
            for j in range(3)
        ],
        axis=1,
    )
    qkv_near = relay_near(qkv_part, F)
    qkv_got = relay_far(qkv_part, qkv_near, F)
    w_qkv = natural(qkv_got).reshape(width, 3 * head_width)

    out_half = lax.dynamic_slice_in_dim(out_weight, me % 2 * head_width, head_width, 0)
    out_mine = lax.all_gather(out_half, "fsdp", axis=0)
    fetched = after(pick(core, gate_weight, up_weight, S, F), qkv_near)
    w_mine = lax.all_to_all(fetched, "fsdp", split_axis=0, concat_axis=0, tiled=True)
    w_mine = w_mine.reshape(width, ff_rows)
    w_other = lax.ppermute(w_mine, "seq", mate)

    tabs = rotary_tables(S * local_len)
    m, a1 = project(x_all, gain1, shift1, w_qkv, bias)
    q, k, v, o = attend(m.reshape(S, seqs, local_len, 3 * head_width), tabs, head_width)
    o_got = lax.all_to_all(o, "seq", split_axis=0, concat_axis=0, tiled=True)
    dy_own = cotangent.reshape(rows, width)
    dy_near = relay_near(after(dy_own, o), F)
    out_other = lax.ppermute(out_mine, "seq", mate)
    o_got = o_got.reshape(S, rows, head_width)

    x_own = tokens.reshape(rows, width)
    x1, a2 = mid(core, o_got, out_mine, out_other, x_own, gain2, shift2)
    a2_all = lax.all_gather(a2, "fsdp", axis=0, tiled=True)
    dy_got = relay_far(dy_own, after(dy_near, a2_all), F)
    first = nn(a2_all, w_mine)
    dy_all = natural(dy_got).reshape(F * rows, width)
    down_half = lax.dynamic_index_in_dim(
        down_weight.reshape(ratio, F, ff_part, width), me % 2, 0, keepdims=False
    )
    down_half = after(down_half, first)
    down_mine = lax.all_to_all(down_half, "fsdp", split_axis=0, concat_axis=0, tiled=True)
    down_other = lax.ppermute(down_mine, "seq", mate)
    second = nn(a2_all, w_other)
    g = jnp.where(even, first, second)
    u = jnp.where(even, second, first)
    sig = jax.nn.sigmoid(g)
    silu = g * sig
    hid = (silu * u).astype(bf16)
    down_grad_part = tn(hid, dy_all).astype(bf16)
    down_grad = lax.psum_scatter(down_grad_part, "seq", scatter_dimension=1, tiled=True)
    down_mine, down_other, dy_late = after((down_mine, down_other, dy_all), down_grad_part)
    w_down = jnp.stack(
        [jnp.where(even, down_mine, down_other), jnp.where(even, down_other, down_mine)], axis=1
    ).reshape(ff_rows, width)
    dh = nt(dy_late, w_down)
    dg = (dh * u * sig * (1.0 + g * (1.0 - sig))).astype(bf16)
    du = (dh * silu).astype(bf16)
    d_first = jnp.where(even, dg, du)
    d_second = jnp.where(even, du, dg)
    dn2_part = (nt(d_first, w_mine) + nt(d_second, w_other)).astype(bf16)
    dn2_part = dn2_part.reshape(F, rows, width)
    dn2_pieces = [
        lax.dynamic_index_in_dim(dn2_part, here ^ j, 0, keepdims=False) for j in range(F)
    ]
    dgu = after(jnp.concatenate([dg, du], axis=1), dn2_pieces)
    dn2_pieces = send_flips(dn2_pieces, F)
    both_part = tn(dgu, a2_all).astype(bf16)
    both_part = both_part.reshape(2, ff_rows, width)
    both = lax.psum_scatter(both_part, "seq", scatter_dimension=1, tiled=True)
    hid_late = after(hid, both_part)
    down_part = nn(hid_late, w_down).astype(bf16)

    dn2_pieces = after(dn2_pieces, down_part)
    dx1, dxl, do_two, gain2_part, shift2_part = mid_back(
        core, dn2_pieces, x1, dy_own, gain2, out_mine, out_other
    )
    do = lax.all_to_all(do_two, "seq", split_axis=0, concat_axis=0, tiled=True)
    do = do.reshape(S, seqs, local_len, head_width)

    dxl_pieces = gather_flips(dxl, F)
    o_got = after(o_got, dxl)
    o_pieces = []
    for j in range(F):
        piece = lax.dynamic_slice_in_dim(o_got, 2 * (here ^ j), 2, 0)
        o_pieces.append(lax.ppermute(piece, "fsdp", flip_pairs(F, j)) if j else piece)

    dm_parts = [g.reshape(all_rows, head_width) for g in attend_back(q, k, v, do, tabs)]
    joint_part = joint(*dm_parts, w_qkv, dxl_pieces, o_pieces)
    joint_sum = lax.psum_scatter(joint_part, "seq", scatter_dimension=0, tiled=True)

    a1_late, dm_parts, both, down_part = after((a1, dm_parts, both, down_part), joint_part)
    dm = jnp.concatenate(dm_parts, axis=1)
    both_pieces = to_rows(both, F, here)
    qkv_part_grad = tn(a1_late, dm).astype(bf16)
    qkv_part_grad = qkv_part_grad.reshape(F, shard, 3 * head_width)
    qkv_pieces = [
        lax.dynamic_index_in_dim(qkv_part_grad, here ^ j, 0, keepdims=False) for j in range(F)
    ]
    down_part, down_grad = after((down_part, down_grad), qkv_pieces)
    qkv_got = send_flips(qkv_pieces, F)
    down_grad = down_grad.reshape(F, ratio * ff_part, head_width)
    down_grad_pieces = send_flips(
        [lax.dynamic_index_in_dim(down_grad, here ^ j, 0, keepdims=False) for j in range(F)], F
    )
    down_part = down_part.reshape(F, rows, width)
    down_pieces = send_flips(
        [lax.dynamic_index_in_dim(down_part, here ^ j, 0, keepdims=False) for j in range(F)], F
    )
    dm_late, dn1_late, x_late = after((dm, joint_part, x_all), qkv_pieces)
    xh_all, _ = norm_stats(x_late.astype(f32))
    dn1_late = dn1_late[:, :width].astype(f32)
    attn_gain_part = jnp.sum(dn1_late * xh_all, axis=0)
    attn_shift_part = jnp.sum(dn1_late, axis=0)
    qkv_got = after(qkv_got, attn_gain_part)
    qkv_sum = total(qkv_got).astype(bf16)
    qkv_result = contiguous_thirds(qkv_sum.reshape(shard, 3, head_width), S, me).astype(f32)
    both_pieces, down_grad_pieces, down_pieces = after(
        (both_pieces, down_grad_pieces, down_pieces), qkv_sum
    )
    both = natural(both_pieces).transpose(1, 0, 2, 3).reshape(2, ff_block, shard).astype(f32)
    gate_result, up_result = both[0].T, both[1].T
    down_result = natural(down_grad_pieces).reshape(F, ratio, ff_part, head_width)
    down_result = down_result.transpose(1, 0, 2, 3).reshape(ff_rows, head_width).astype(f32)
    layer_out = (x1 + total(down_pieces)).astype(bf16).reshape(tokens.shape)
    joint_sum = after(joint_sum, qkv_sum, layer_out, gate_result, up_result, down_result)
    dn1 = joint_sum[:, :width].astype(f32)
    out_result = joint_sum[:, width:].T.astype(f32)

    bias_part = jnp.sum(dm_late, axis=0, dtype=f32).reshape(3, 1, head_width)
    bias_full = lax.dynamic_update_slice_in_dim(
        jnp.zeros((3, S, head_width), f32), bias_part, me, 1
    ).reshape(3 * width)
    small_parts = [
        attn_gain_part,
        attn_shift_part,
        bias_full[: 2 * width],
        bias_full[2 * width :],
        gain2_part[0],
        shift2_part[0],
    ]
    packed = jnp.concatenate([p.reshape(devices, -1) for p in small_parts], axis=1)
    packed = lax.all_to_all(packed, MESH_AXES, split_axis=0, concat_axis=0, tiled=True)
    xh, r = norm_stats(x_own.astype(f32))
    tokens_grad = (dx1 + norm_back(dn1, xh, r, gain1)).reshape(tokens.shape)
    packed = jnp.sum(after(packed, tokens_grad), axis=0)
    results = []
    start = 0
    for p in small_parts:
        size = p.shape[0] // devices
        results.append(packed[start : start + size])
        start += size
    gain1_result, shift1_result, bias_result, value_result, gain2_result, shift2_result = results

    return (
        layer_out,
        tokens_grad,
        gain1_result,
        shift1_result,
        qkv_result,
        bias_result,
        value_result,
        out_result,
        gain2_result,
        shift2_result,
        gate_result,
        up_result,
        down_result,
    )


def solution(mesh):
    return jax.shard_map(
        on_device,
        mesh=mesh,
        in_specs=(
            P("fsdp", "seq", None),
            P("fsdp"),
            P("fsdp"),
            P("fsdp", None),
            P("fsdp"),
            P("fsdp", None),
            P("fsdp"),
            P("fsdp"),
            P("fsdp", None),
            P("fsdp", None),
            P("fsdp", None),
            P("fsdp", "seq", None),
        ),
        out_specs=(
            P("fsdp", "seq", None),
            P("fsdp", "seq", None),
            P(("seq", "fsdp")),
            P(("seq", "fsdp")),
            P("fsdp", "seq"),
            P(("seq", "fsdp")),
            P(("seq", "fsdp")),
            P("fsdp", "seq"),
            P(("seq", "fsdp")),
            P(("seq", "fsdp")),
            P("fsdp", "seq"),
            P("fsdp", "seq"),
            P("fsdp", "seq"),
        ),
        check_vma=False,
    )
```

```python
import functools

import jax
import jax.numpy as jnp
from jax import lax
from jax.experimental import pallas as pl
from jax.experimental.pallas import tpu as pltpu
from jax.sharding import PartitionSpec as P


HD = 64
ROT = 16
PAIR = 2 * HD
MESH_AXES = ("seq", "fsdp")


def nn(a, b):
    return lax.dot_general(a, b, (((1,), (0,)), ((), ())), preferred_element_type=jnp.float32)


def nt(a, b):
    return lax.dot_general(a, b, (((1,), (1,)), ((), ())), preferred_element_type=jnp.float32)


def tn(a, b):
    return lax.dot_general(a, b, (((0,), (0,)), ((), ())), preferred_element_type=jnp.float32)


def norm_stats(x):
    mean = jnp.mean(x, axis=-1, keepdims=True)
    center = x - mean
    var = jnp.mean(center * center, axis=-1, keepdims=True)
    r = lax.rsqrt(var + 1e-05)
    return center * r, r


def norm_back(dn, xh, r, gain):
    e = dn * gain
    return r * (
        e
        - jnp.mean(e, axis=-1, keepdims=True)
        - xh * jnp.mean(e * xh, axis=-1, keepdims=True)
    )


def rotary_tables(length):
    lane = jnp.arange(PAIR) % HD
    ladder = 10000.0 ** (-jnp.arange(0, ROT, 2, dtype=jnp.float32) / ROT)
    places = jnp.arange(length, dtype=jnp.float32)
    angles = places[:, None] * jnp.tile(ladder, PAIR // (ROT // 2))[None, :]
    first = (lane < ROT // 2)[None, :]
    second = ((lane >= ROT // 2) & (lane < ROT))[None, :]
    cos_tab = jnp.where(first | second, jnp.cos(angles), 1.0)
    sine = jnp.sin(angles)
    return cos_tab, jnp.where(first, -sine, 0.0), jnp.where(second, sine, 0.0)


def rotate(x, cos_tab, minus, plus):
    ahead = pltpu.roll(x, PAIR - ROT // 2, 1)
    behind = pltpu.roll(x, ROT // 2, 1)
    return x * cos_tab + ahead * minus + behind * plus


def head_lanes(x, head):
    lane = lax.broadcasted_iota(jnp.int32, x.shape, 1)
    return jnp.where((lane < HD) == (head == 0), x, jnp.zeros_like(x))


def transposed(x):
    return x.astype(jnp.float32).T.astype(x.dtype)


def causal_exp(scores, row_block, block):
    e = jnp.exp(scores)
    if row_block:
        done = e[: row_block * block]
    last = e[row_block * block :]
    key = lax.broadcasted_iota(jnp.int32, last.shape, 0)
    query = lax.broadcasted_iota(jnp.int32, last.shape, 1)
    last = jnp.where(key <= query, last, 0.0)
    return jnp.concatenate([done, last], axis=0) if row_block else last


def attend_kernel(block, mq, mk, mv, cos_ref, minus_ref, plus_ref, q_out, k_out, v_out, o_out):
    shape = q_out.shape
    length = shape[0] * shape[2]
    tabs = (cos_ref[...], minus_ref[...], plus_ref[...])
    q = rotate(mq[...].reshape(length, PAIR), *tabs).astype(jnp.bfloat16)
    k = rotate(mk[...].reshape(length, PAIR), *tabs).astype(jnp.bfloat16)
    v = mv[...].reshape(length, PAIR).astype(jnp.bfloat16)
    q_out[...] = q.reshape(shape)
    k_out[...] = k.reshape(shape)
    v_out[...] = v.reshape(shape)
    qs = q * jnp.bfloat16(HD**-0.5)
    vt = transposed(v)
    q_heads = [head_lanes(qs, h) for h in range(2)]
    rows = []
    for i in range(length // block):
        n = (i + 1) * block
        both = []
        for h in range(2):
            e = causal_exp(nt(k[:n], q_heads[h][i * block : n]), i, block)
            inv = 1.0 / jnp.sum(e, axis=0, keepdims=True)
            p = (e * inv).astype(jnp.bfloat16)
            both.append(nn(vt[h * HD : (h + 1) * HD, :n], p))
        rows.append(jnp.concatenate(both, axis=0).T)
    o_out[...] = jnp.concatenate(rows, axis=0).astype(jnp.bfloat16).reshape(shape)


def attend_back_kernel(block, q_ref, k_ref, v_ref, do_ref, cos_ref, minus_ref, plus_ref,
                       dq_out, dk_out, dv_out, dk_acc, dv_acc):
    shape = dq_out.shape
    length = shape[0] * shape[2]
    tabs = (cos_ref[...], -minus_ref[...], -plus_ref[...])
    scale = HD**-0.5
    q = q_ref[...].reshape(length, PAIR) * jnp.bfloat16(scale)
    k = k_ref[...].reshape(length, PAIR)
    v = v_ref[...].reshape(length, PAIR)
    do = do_ref[...].reshape(length, PAIR)
    kt = transposed(k)
    q_heads = [head_lanes(q, h) for h in range(2)]
    do_heads = [head_lanes(do, h) for h in range(2)]
    dk_acc[...] = jnp.zeros_like(dk_acc)
    dv_acc[...] = jnp.zeros_like(dv_acc)
    rows = []
    for i in range(length // block):
        n = (i + 1) * block
        both = []
        for h in range(2):
            q_i = q_heads[h][i * block : n]
            do_i = do_heads[h][i * block : n]
            e = causal_exp(nt(k[:n], q_i), i, block)
            p = e * (1.0 / jnp.sum(e, axis=0, keepdims=True))
            dp = nt(v[:n], do_i)
            inner = jnp.sum(p * dp, axis=0, keepdims=True)
            ds = (p * (dp - inner)).astype(jnp.bfloat16)
            dv_acc[:n] += nn(p.astype(jnp.bfloat16), do_i)
            dk_acc[:n] += nn(ds, q_i)
            both.append(nn(kt[h * HD : (h + 1) * HD, :n], ds))
        rows.append(jnp.concatenate(both, axis=0).T)

    def finish(g):
        return g.astype(jnp.bfloat16).astype(jnp.float32)

    dq = finish(jnp.concatenate(rows, axis=0) * scale)
    dq_out[...] = rotate(dq, *tabs).astype(jnp.bfloat16).reshape(shape)
    dk_out[...] = rotate(finish(dk_acc[...]), *tabs).astype(jnp.bfloat16).reshape(shape)
    dv_out[...] = dv_acc[...].astype(jnp.bfloat16).reshape(shape)


def attention_specs(parts, seqs, local_len, width):
    pairs = width // PAIR

    def spec(offset):
        return pl.BlockSpec((parts, 1, local_len, PAIR), lambda i, j: (0, i, 0, offset * pairs + j))

    length = parts * local_len
    tab = pl.BlockSpec((length, PAIR), lambda i, j: (0, 0))
    return spec, tab, (seqs, pairs), min(256, length)


def attend(m, tabs, width):
    parts, seqs, local_len, _ = m.shape
    spec, tab, grid, block = attention_specs(parts, seqs, local_len, width)
    out = jax.ShapeDtypeStruct((parts, seqs, local_len, width), jnp.bfloat16)
    work = seqs * (width // HD) * (parts * local_len) ** 2
    return pl.pallas_call(
        functools.partial(attend_kernel, block),
        grid=grid,
        in_specs=[spec(0), spec(1), spec(2), tab, tab, tab],
        out_specs=[spec(0)] * 4,
        out_shape=[out] * 4,
        compiler_params=pltpu.CompilerParams(vmem_limit_bytes=48 << 20),
        cost_estimate=pl.CostEstimate(
            flops=work * HD * 4, bytes_accessed=m.size * 4 + out.size * 8, transcendentals=work
        ),
        name="attend",
    )(m, m, m, *tabs)


def attend_back(q, k, v, do, tabs):
    parts, seqs, local_len, width = q.shape
    spec, tab, grid, block = attention_specs(parts, seqs, local_len, width)
    out = jax.ShapeDtypeStruct(q.shape, jnp.bfloat16)
    length = parts * local_len
    work = seqs * (width // HD) * length**2
    return pl.pallas_call(
        functools.partial(attend_back_kernel, block),
        grid=grid,
        in_specs=[spec(0)] * 4 + [tab] * 3,
        out_specs=[spec(0)] * 3,
        out_shape=[out] * 3,
        scratch_shapes=[pltpu.VMEM((length, PAIR), jnp.float32)] * 2,
        compiler_params=pltpu.CompilerParams(vmem_limit_bytes=48 << 20),
        cost_estimate=pl.CostEstimate(
            flops=work * HD * 10, bytes_accessed=out.size * 14, transcendentals=work
        ),
        name="attend_back",
    )(q, k, v, do, *tabs)


def mid_kernel(core_ref, o_ref, mine_ref, other_ref, x_ref, gain_ref, shift_ref, x1_out, a_out):
    step = pl.program_id(0)
    core = core_ref[0]

    @pl.when(step == 0)
    def _():
        x1_out[...] = x_ref[...].astype(jnp.float32)

    x1_out[...] += nn(o_ref[core], mine_ref[0]) + nn(o_ref[1 - core], other_ref[0])

    @pl.when(step == pl.num_programs(0) - 1)
    def _():
        xh, _ = norm_stats(x1_out[...])
        a_out[...] = (xh * gain_ref[...] + shift_ref[...]).astype(jnp.bfloat16)


def mid(core, o, mine, other, x, gain, shift):
    parts, rows, head_width = o.shape
    width = x.shape[1]
    whole = lambda shape: pl.BlockSpec(shape, lambda i, c: (0, 0))
    return pl.pallas_call(
        mid_kernel,
        grid_spec=pltpu.PrefetchScalarGridSpec(
            num_scalar_prefetch=1,
            grid=(parts // 2,),
            in_specs=[
                pl.BlockSpec((2, rows, head_width), lambda i, c: (i, 0, 0)),
                pl.BlockSpec((1, head_width, width), lambda i, c: (i, 0, 0)),
                pl.BlockSpec((1, head_width, width), lambda i, c: (i, 0, 0)),
                whole((rows, width)),
                whole((1, width)),
                whole((1, width)),
            ],
            out_specs=[whole((rows, width)), whole((rows, width))],
        ),
        out_shape=[
            jax.ShapeDtypeStruct((rows, width), jnp.float32),
            jax.ShapeDtypeStruct((rows, width), jnp.bfloat16),
        ],
        compiler_params=pltpu.CompilerParams(vmem_limit_bytes=48 << 20),
        cost_estimate=pl.CostEstimate(
            flops=2 * rows * width * width,
            bytes_accessed=2 * width * width + 10 * rows * width,
            transcendentals=0,
        ),
        name="mid",
    )(core, o, mine, other, x, gain[None, :], shift[None, :])


def mid_back_kernel(count, core_ref, *refs):
    pieces = refs[:count]
    x1_ref, dy_ref, gain_ref, mine_ref, other_ref = refs[count : count + 5]
    dx1_out, dxl_out, do_out, gain_out, shift_out = refs[count + 5 :]
    core = core_ref[0]

    @pl.when(pl.program_id(0) == 0)
    def _():
        dn = pieces[0][...].astype(jnp.float32)
        for piece in pieces[1:]:
            dn = dn + piece[...].astype(jnp.float32)
        xh, r = norm_stats(x1_ref[...])
        gain_out[...] = jnp.sum(dn * xh, axis=0, keepdims=True)
        shift_out[...] = jnp.sum(dn, axis=0, keepdims=True)
        dx1 = dy_ref[...].astype(jnp.float32) + norm_back(dn, xh, r, gain_ref[...])
        dx1_out[...] = dx1
        dxl_out[...] = dx1.astype(jnp.bfloat16)

    dxl = dxl_out[...]
    do_out[core] = nt(dxl, mine_ref[0]).astype(jnp.bfloat16)
    do_out[1 - core] = nt(dxl, other_ref[0]).astype(jnp.bfloat16)


def mid_back(core, pieces, x1, dy, gain, mine, other):
    rows, width = x1.shape
    halves, head_width, _ = mine.shape
    whole = lambda shape: pl.BlockSpec(shape, lambda i, c: (0, 0))
    full = whole((rows, width))
    weight = pl.BlockSpec((1, head_width, width), lambda i, c: (i, 0, 0))
    return pl.pallas_call(
        functools.partial(mid_back_kernel, len(pieces)),
        grid_spec=pltpu.PrefetchScalarGridSpec(
            num_scalar_prefetch=1,
            grid=(halves,),
            in_specs=[full] * (len(pieces) + 2) + [whole((1, width)), weight, weight],
            out_specs=[
                full,
                full,
                pl.BlockSpec((2, rows, head_width), lambda i, c: (i, 0, 0)),
                whole((1, width)),
                whole((1, width)),
            ],
        ),
        out_shape=[
            jax.ShapeDtypeStruct((rows, width), jnp.float32),
            jax.ShapeDtypeStruct((rows, width), jnp.bfloat16),
            jax.ShapeDtypeStruct((2 * halves, rows, head_width), jnp.bfloat16),
            jax.ShapeDtypeStruct((1, width), jnp.float32),
            jax.ShapeDtypeStruct((1, width), jnp.float32),
        ],
        compiler_params=pltpu.CompilerParams(vmem_limit_bytes=56 << 20),
        cost_estimate=pl.CostEstimate(
            flops=2 * rows * width * width,
            bytes_accessed=2 * width * width + 20 * rows * width,
            transcendentals=0,
        ),
        name="mid_back",
    )(core, *pieces, x1, dy, gain[None, :], mine, other)


def joint_kernel(count, *refs):
    dq_ref, dk_ref, dv_ref, w_ref = refs[:4]
    x_refs = refs[4 : 4 + count]
    o_refs = refs[4 + count : 4 + 2 * count]
    out_ref = refs[-1]
    width, cols = w_ref.shape
    part = cols // 3
    w = w_ref[...]
    total = nt(dq_ref[...], w[:, :part])
    total = total + nt(dk_ref[...], w[:, part : 2 * part])
    total = total + nt(dv_ref[...], w[:, 2 * part :])
    out_ref[:, :width] = total.astype(jnp.bfloat16)
    for h in range(2):
        side = tn(x_refs[0][...], o_refs[0][h])
        for x_ref, o_ref in zip(x_refs[1:], o_refs[1:]):
            side = side + tn(x_ref[...], o_ref[h])
        start = width + h * part
        out_ref[:, start : start + part] = side.astype(jnp.bfloat16)


def joint(dq, dk, dv, w, xs, os):
    all_rows, part = dq.shape
    width, cols = w.shape
    rows = xs[0].shape[0]
    count = len(xs)
    parts = width // part
    block = all_rows // parts
    if block != part:
        raise ValueError("unsupported shape")
    row_block = pl.BlockSpec((block, part), lambda i: (i, 0))
    return pl.pallas_call(
        functools.partial(joint_kernel, count),
        grid=(parts,),
        in_specs=[row_block] * 3
        + [pl.BlockSpec((width, cols), lambda i: (0, 0))]
        + [pl.BlockSpec((rows, part), lambda i: (0, i))] * count
        + [pl.BlockSpec((2, rows, part), lambda i: (0, 0, 0))] * count,
        out_specs=pl.BlockSpec((block, width + 2 * part), lambda i: (i, 0)),
        out_shape=jax.ShapeDtypeStruct((all_rows, width + 2 * part), jnp.bfloat16),
        compiler_params=pltpu.CompilerParams(vmem_limit_bytes=48 << 20),
        cost_estimate=pl.CostEstimate(
            flops=2 * all_rows * width * cols + 4 * count * rows * width * part,
            bytes_accessed=4 * all_rows * (width + cols) + 2 * width * cols,
            transcendentals=0,
        ),
        name="joint",
    )(dq, dk, dv, w, *xs, *os)


def pick_kernel(counts, core_ref, gate_ref, up_ref, out_ref):
    blocks, fsdp_parts, part = counts

    def pick(source):
        rows = source[...]
        for f in range(fsdp_parts):
            starts = [(t * fsdp_parts + f) * part for t in range(blocks)]
            out_ref[f] = jnp.concatenate([rows[:, a : a + part] for a in starts], axis=1)

    @pl.when(core_ref[0] == 0)
    def _():
        pick(gate_ref)

    @pl.when(core_ref[0] != 0)
    def _():
        pick(up_ref)


def pick(core, gate, up, blocks, fsdp_parts):
    rows, cols = gate.shape
    part = cols // (blocks * fsdp_parts)
    block = min(64, rows)
    return pl.pallas_call(
        functools.partial(pick_kernel, (blocks, fsdp_parts, part)),
        grid_spec=pltpu.PrefetchScalarGridSpec(
            num_scalar_prefetch=1,
            grid=(rows // block,),
            in_specs=[
                pl.BlockSpec((block, cols), lambda i, c: (jnp.where(c[0] == 0, i, 0), 0)),
                pl.BlockSpec((block, cols), lambda i, c: (jnp.where(c[0] == 0, 0, i), 0)),
            ],
            out_specs=pl.BlockSpec((fsdp_parts, block, blocks * part), lambda i, c: (0, i, 0)),
        ),
        out_shape=jax.ShapeDtypeStruct((fsdp_parts, rows, blocks * part), gate.dtype),
        compiler_params=pltpu.CompilerParams(vmem_limit_bytes=32 << 20),
        cost_estimate=pl.CostEstimate(flops=0, bytes_accessed=4 * rows * cols, transcendentals=0),
        name="pick",
    )(core, gate, up)


def third_rounds(parts):
    left = {s: [(j, (j * parts + s) // 3, (j * parts + s) % 3) for j in range(3)] for s in range(parts)}
    rounds = []
    for _ in range(3):
        owner = {}

        def place(s, seen):
            for edge in left[s]:
                d = edge[1]
                if d in seen:
                    continue
                seen.add(d)
                if d not in owner or place(owner[d][0], seen):
                    owner[d] = (s, edge)
                    return True
            return False

        for s in range(parts):
            place(s, set())
        send = [0] * parts
        slot = [0] * parts
        pairs = []
        for d, (s, edge) in owner.items():
            left[s].remove(edge)
            send[s] = edge[0]
            slot[d] = edge[2]
            pairs.append((s, d))
        rounds.append((sorted(pairs), send, slot))
    return rounds


def contiguous_thirds(block, parts, me):
    got = []
    slots = []
    for pairs, send, slot in third_rounds(parts):
        piece = lax.dynamic_index_in_dim(block, jnp.array(send)[me], 1, keepdims=False)
        got.append(lax.ppermute(piece, "seq", pairs))
        slots.append(jnp.array(slot)[me])
    out = []
    for k in range(3):
        out.append(jnp.where(slots[0] == k, got[0], jnp.where(slots[1] == k, got[1], got[2])))
    return jnp.concatenate(out, axis=1)


def after(x, *done):
    return lax.optimization_barrier((x, *done))[0]


def flip_pairs(parts, j):
    return [(i, i ^ j) for i in range(parts)]


def gather_flips(block, parts):
    return [block] + [lax.ppermute(block, "fsdp", flip_pairs(parts, j)) for j in range(1, parts)]


def relay_near(block, parts):
    if parts != 4:
        return gather_flips(block, parts)[1:]
    return [lax.ppermute(block, "fsdp", flip_pairs(parts, j)) for j in (1, 2)]


def relay_far(block, near, parts):
    if parts != 4:
        return [block, *near]
    one, two = near
    half = block.shape[0] // 2
    head = lax.ppermute(two[:half], "fsdp", flip_pairs(parts, 1))
    tail = lax.ppermute(one[half:], "fsdp", flip_pairs(parts, 2))
    return [block, one, two, (head, tail)]


def send_flips(pieces, parts):
    return [pieces[0]] + [
        lax.ppermute(pieces[j], "fsdp", flip_pairs(parts, j)) for j in range(1, parts)
    ]


def total(pieces):
    out = pieces[0].astype(jnp.float32)
    for piece in pieces[1:]:
        out = out + piece.astype(jnp.float32)
    return out


def project_kernel(x_ref, gain_ref, shift_ref, w_ref, bias_ref, m_out, a_out):
    x = x_ref[...].astype(jnp.float32)
    xh, _ = norm_stats(x)
    a = (xh * gain_ref[...] + shift_ref[...]).astype(jnp.bfloat16)
    a_out[...] = a
    m_out[...] = nn(a, w_ref[...]) + bias_ref[...]


def project(x, gain, shift, w, bias):
    rows, width = x.shape
    cols = w.shape[1]
    block = min(256, rows)
    whole = lambda shape: pl.BlockSpec(shape, lambda i: (0, 0))
    return pl.pallas_call(
        project_kernel,
        grid=(rows // block,),
        in_specs=[
            pl.BlockSpec((block, width), lambda i: (i, 0)),
            whole((1, width)),
            whole((1, width)),
            whole((width, cols)),
            whole((1, cols)),
        ],
        out_specs=[
            pl.BlockSpec((block, cols), lambda i: (i, 0)),
            pl.BlockSpec((block, width), lambda i: (i, 0)),
        ],
        out_shape=[
            jax.ShapeDtypeStruct((rows, cols), jnp.float32),
            jax.ShapeDtypeStruct((rows, width), jnp.bfloat16),
        ],
        compiler_params=pltpu.CompilerParams(vmem_limit_bytes=48 << 20),
        cost_estimate=pl.CostEstimate(
            flops=2 * rows * width * cols,
            bytes_accessed=rows * width * 4 + rows * cols * 4 + width * cols * 2,
            transcendentals=0,
        ),
        name="project",
    )(x, gain[None, :], shift[None, :], w, bias[None, :])


def to_rows(block, fsdp_parts, here):
    rows = block.shape[2] // fsdp_parts
    pieces = []
    for j in range(fsdp_parts):
        piece = lax.dynamic_slice_in_dim(block, (here ^ j) * rows, rows, 2)
        pieces.append(lax.ppermute(piece, "fsdp", flip_pairs(fsdp_parts, j)) if j else piece)
    return pieces


def on_device(
    tokens,
    attn_gain,
    attn_shift,
    qkv_weight,
    qkv_bias,
    out_weight,
    ffn_gain,
    ffn_shift,
    gate_weight,
    up_weight,
    down_weight,
    cotangent,
):
    f32, bf16 = jnp.float32, jnp.bfloat16
    seqs, local_len, width = tokens.shape
    S = lax.axis_size("seq")
    F = lax.axis_size("fsdp")
    me = lax.axis_index("seq")
    devices = S * F
    rows = seqs * local_len
    all_rows = S * rows
    head_width = width // S
    ff_rows, _ = down_weight.shape
    shard = width // F

    ratio = S // F
    if ratio != 2 or F & (F - 1):
        raise ValueError("unsupported mesh")
    ff_block = F * ff_rows // S
    ff_part = ff_block // F
    even = me % 2 == 0
    core = (me % 2).reshape(1).astype(jnp.int32)
    mate = flip_pairs(S, 1)
    here = lax.axis_index("fsdp")

    def natural(pieces):
        out = jnp.zeros((F, *pieces[0].shape), pieces[0].dtype)
        rest = (0,) * (pieces[0].ndim - 1)
        for j, piece in enumerate(pieces):
            start = 0
            for part in piece if isinstance(piece, tuple) else (piece,):
                out = lax.dynamic_update_slice(out, part[None], (here ^ j, start, *rest))
                start += part.shape[0]
        return out

    x_all = lax.all_gather(tokens, "seq", axis=0).reshape(all_rows, width)
    small = jnp.concatenate([attn_gain, attn_shift, ffn_gain, ffn_shift, qkv_bias])
    small = natural(gather_flips(small, F))
    params = [small[:, i * shard : (i + 1) * shard].reshape(width).astype(f32) for i in range(4)]
    gain1, shift1, gain2, shift2 = params
    bias = small[:, 4 * shard :].reshape(3, S, head_width).astype(f32)
    bias = lax.dynamic_index_in_dim(bias, me, 1, keepdims=False).reshape(3 * head_width)
    qkv_part = jnp.concatenate(
        [
            lax.dynamic_slice_in_dim(qkv_weight, j * width + me * head_width, head_width, 1)
            for j in range(3)
        ],
        axis=1,
    )
    qkv_near = relay_near(qkv_part, F)
    qkv_got = relay_far(qkv_part, qkv_near, F)
    w_qkv = natural(qkv_got).reshape(width, 3 * head_width)

    out_half = lax.dynamic_slice_in_dim(out_weight, me % 2 * head_width, head_width, 0)
    out_mine = lax.all_gather(out_half, "fsdp", axis=0)
    fetched = after(pick(core, gate_weight, up_weight, S, F), qkv_near)
    w_mine = lax.all_to_all(fetched, "fsdp", split_axis=0, concat_axis=0, tiled=True)
    w_mine = w_mine.reshape(width, ff_rows)
    w_other = lax.ppermute(w_mine, "seq", mate)

    tabs = rotary_tables(S * local_len)
    m, a1 = project(x_all, gain1, shift1, w_qkv, bias)
    q, k, v, o = attend(m.reshape(S, seqs, local_len, 3 * head_width), tabs, head_width)
    o_got = lax.all_to_all(o, "seq", split_axis=0, concat_axis=0, tiled=True)
    dy_own = cotangent.reshape(rows, width)
    dy_near = relay_near(after(dy_own, o), F)
    out_other = lax.ppermute(out_mine, "seq", mate)
    o_got = o_got.reshape(S, rows, head_width)

    x_own = tokens.reshape(rows, width)
    x1, a2 = mid(core, o_got, out_mine, out_other, x_own, gain2, shift2)
    a2_near = relay_near(a2, F)
    a2_got = relay_far(a2, a2_near, F)
    a2_all = natural(a2_got).reshape(F * rows, width)
    dy_got = relay_far(dy_own, after(dy_near, a2_all), F)
    first = nn(a2_all, w_mine)
    dy_all = natural(dy_got).reshape(F * rows, width)
    down_half = lax.dynamic_index_in_dim(
        down_weight.reshape(ratio, F, ff_part, width), me % 2, 0, keepdims=False
    )
    down_half = after(down_half, first)
    down_mine = lax.all_to_all(down_half, "fsdp", split_axis=0, concat_axis=0, tiled=True)
    down_other = lax.ppermute(down_mine, "seq", mate)
    second = nn(a2_all, w_other)
    g = jnp.where(even, first, second)
    u = jnp.where(even, second, first)
    sig = jax.nn.sigmoid(g)
    silu = g * sig
    hid = (silu * u).astype(bf16)
    down_grad_part = tn(hid, dy_all).astype(bf16)
    down_grad = lax.psum_scatter(down_grad_part, "seq", scatter_dimension=1, tiled=True)
    down_mine, down_other, dy_late = after((down_mine, down_other, dy_all), down_grad_part)
    w_down = jnp.stack(
        [jnp.where(even, down_mine, down_other), jnp.where(even, down_other, down_mine)], axis=1
    ).reshape(ff_rows, width)
    dh = nt(dy_late, w_down)
    dg = (dh * u * sig * (1.0 + g * (1.0 - sig))).astype(bf16)
    du = (dh * silu).astype(bf16)
    d_first = jnp.where(even, dg, du)
    d_second = jnp.where(even, du, dg)
    dn2_part = (nt(d_first, w_mine) + nt(d_second, w_other)).astype(bf16)
    dn2_part = dn2_part.reshape(F, rows, width)
    dn2_pieces = [
        lax.dynamic_index_in_dim(dn2_part, here ^ j, 0, keepdims=False) for j in range(F)
    ]
    dgu = after(jnp.concatenate([dg, du], axis=1), dn2_pieces)
    dn2_pieces = send_flips(dn2_pieces, F)
    both_part = tn(dgu, a2_all).astype(bf16)
    both_part = both_part.reshape(2, ff_rows, width)
    both = lax.psum_scatter(both_part, "seq", scatter_dimension=1, tiled=True)
    hid_late = after(hid, both_part)
    down_part = nn(hid_late, w_down).astype(bf16).reshape(F, rows, width)
    down_out = [lax.dynamic_index_in_dim(down_part, here ^ j, 0, keepdims=False) for j in range(F)]

    dn2_pieces = after(dn2_pieces, down_out)
    dx1, dxl, do_two, gain2_part, shift2_part = mid_back(
        core, dn2_pieces, x1, dy_own, gain2, out_mine, out_other
    )
    do = lax.all_to_all(do_two, "seq", split_axis=0, concat_axis=0, tiled=True)
    do = do.reshape(S, seqs, local_len, head_width)

    dxl_pieces = gather_flips(dxl, F)
    o_got = after(o_got, dxl)
    o_pieces = []
    for j in range(F):
        piece = lax.dynamic_slice_in_dim(o_got, 2 * (here ^ j), 2, 0)
        o_pieces.append(lax.ppermute(piece, "fsdp", flip_pairs(F, j)) if j else piece)

    dm_parts = [g.reshape(all_rows, head_width) for g in attend_back(q, k, v, do, tabs)]
    down_out = after(down_out, dm_parts)
    down_pieces = send_flips(down_out, F)
    joint_part = joint(*dm_parts, w_qkv, dxl_pieces, o_pieces)
    joint_sum = lax.psum_scatter(joint_part, "seq", scatter_dimension=0, tiled=True)

    a1_late, dm_parts, both = after((a1, dm_parts, both), joint_part)
    dm = jnp.concatenate(dm_parts, axis=1)
    both_pieces = to_rows(both, F, here)
    qkv_part_grad = tn(a1_late, dm).astype(bf16)
    qkv_part_grad = qkv_part_grad.reshape(F, shard, 3 * head_width)
    qkv_pieces = [
        lax.dynamic_index_in_dim(qkv_part_grad, here ^ j, 0, keepdims=False) for j in range(F)
    ]
    down_grad = after(down_grad, qkv_pieces)
    qkv_got = send_flips(qkv_pieces, F)
    down_grad = down_grad.reshape(F, ratio * ff_part, head_width)
    down_grad_pieces = send_flips(
        [lax.dynamic_index_in_dim(down_grad, here ^ j, 0, keepdims=False) for j in range(F)], F
    )
    dm_late, dn1_late, x_late = after((dm, joint_part, x_all), qkv_pieces)
    xh_all, _ = norm_stats(x_late.astype(f32))
    dn1_late = dn1_late[:, :width].astype(f32)
    attn_gain_part = jnp.sum(dn1_late * xh_all, axis=0)
    attn_shift_part = jnp.sum(dn1_late, axis=0)
    qkv_got = after(qkv_got, attn_gain_part)
    qkv_sum = total(qkv_got).astype(bf16)
    qkv_result = contiguous_thirds(qkv_sum.reshape(shard, 3, head_width), S, me).astype(f32)
    both_pieces, down_grad_pieces, down_pieces = after(
        (both_pieces, down_grad_pieces, down_pieces), qkv_sum
    )
    both = natural(both_pieces).transpose(1, 0, 2, 3).reshape(2, ff_block, shard).astype(f32)
    gate_result, up_result = both[0].T, both[1].T
    down_result = natural(down_grad_pieces).reshape(F, ratio, ff_part, head_width)
    down_result = down_result.transpose(1, 0, 2, 3).reshape(ff_rows, head_width).astype(f32)
    layer_out = (x1 + total(down_pieces)).astype(bf16).reshape(tokens.shape)
    joint_sum = after(joint_sum, qkv_sum, layer_out, gate_result, up_result, down_result)
    dn1 = joint_sum[:, :width].astype(f32)
    out_result = joint_sum[:, width:].T.astype(f32)

    bias_part = jnp.sum(dm_late, axis=0, dtype=f32).reshape(3, 1, head_width)
    bias_full = lax.dynamic_update_slice_in_dim(
        jnp.zeros((3, S, head_width), f32), bias_part, me, 1
    ).reshape(3 * width)
    small_parts = [
        attn_gain_part,
        attn_shift_part,
        bias_full[: 2 * width],
        bias_full[2 * width :],
        gain2_part[0],
        shift2_part[0],
    ]
    packed = jnp.concatenate([p.reshape(devices, -1) for p in small_parts], axis=1)
    packed = lax.all_to_all(packed, MESH_AXES, split_axis=0, concat_axis=0, tiled=True)
    xh, r = norm_stats(x_own.astype(f32))
    tokens_grad = (dx1 + norm_back(dn1, xh, r, gain1)).reshape(tokens.shape)
    packed = jnp.sum(after(packed, tokens_grad), axis=0)
    results = []
    start = 0
    for p in small_parts:
        size = p.shape[0] // devices
        results.append(packed[start : start + size])
        start += size
    gain1_result, shift1_result, bias_result, value_result, gain2_result, shift2_result = results

    return (
        layer_out,
        tokens_grad,
        gain1_result,
        shift1_result,
        qkv_result,
        bias_result,
        value_result,
        out_result,
        gain2_result,
        shift2_result,
        gate_result,
        up_result,
        down_result,
    )


def solution(mesh):
    return jax.shard_map(
        on_device,
        mesh=mesh,
        in_specs=(
            P("fsdp", "seq", None),
            P("fsdp"),
            P("fsdp"),
            P("fsdp", None),
            P("fsdp"),
            P("fsdp", None),
            P("fsdp"),
            P("fsdp"),
            P("fsdp", None),
            P("fsdp", None),
            P("fsdp", None),
            P("fsdp", "seq", None),
        ),
        out_specs=(
            P("fsdp", "seq", None),
            P("fsdp", "seq", None),
            P(("seq", "fsdp")),
            P(("seq", "fsdp")),
            P("fsdp", "seq"),
            P(("seq", "fsdp")),
            P(("seq", "fsdp")),
            P("fsdp", "seq"),
            P(("seq", "fsdp")),
            P(("seq", "fsdp")),
            P("fsdp", "seq"),
            P("fsdp", "seq"),
            P("fsdp", "seq"),
        ),
        check_vma=False,
    )
```

```python
import functools

import jax
import jax.numpy as jnp
from jax import lax
from jax.experimental import pallas as pl
from jax.experimental.pallas import tpu as pltpu
from jax.sharding import PartitionSpec as P


HD = 64
ROT = 16
PAIR = 2 * HD
MESH_AXES = ("seq", "fsdp")


def nn(a, b):
    return lax.dot_general(a, b, (((1,), (0,)), ((), ())), preferred_element_type=jnp.float32)


def nt(a, b):
    return lax.dot_general(a, b, (((1,), (1,)), ((), ())), preferred_element_type=jnp.float32)


def tn(a, b):
    return lax.dot_general(a, b, (((0,), (0,)), ((), ())), preferred_element_type=jnp.float32)


def norm_stats(x):
    mean = jnp.mean(x, axis=-1, keepdims=True)
    center = x - mean
    var = jnp.mean(center * center, axis=-1, keepdims=True)
    r = lax.rsqrt(var + 1e-05)
    return center * r, r


def norm_back(dn, xh, r, gain):
    e = dn * gain
    return r * (
        e
        - jnp.mean(e, axis=-1, keepdims=True)
        - xh * jnp.mean(e * xh, axis=-1, keepdims=True)
    )


def rotary_tables(length):
    lane = jnp.arange(PAIR) % HD
    ladder = 10000.0 ** (-jnp.arange(0, ROT, 2, dtype=jnp.float32) / ROT)
    places = jnp.arange(length, dtype=jnp.float32)
    angles = places[:, None] * jnp.tile(ladder, PAIR // (ROT // 2))[None, :]
    first = (lane < ROT // 2)[None, :]
    second = ((lane >= ROT // 2) & (lane < ROT))[None, :]
    cos_tab = jnp.where(first | second, jnp.cos(angles), 1.0)
    sine = jnp.sin(angles)
    return cos_tab, jnp.where(first, -sine, 0.0), jnp.where(second, sine, 0.0)


def rotate(x, cos_tab, minus, plus):
    ahead = pltpu.roll(x, PAIR - ROT // 2, 1)
    behind = pltpu.roll(x, ROT // 2, 1)
    return x * cos_tab + ahead * minus + behind * plus


def head_lanes(x, head):
    lane = lax.broadcasted_iota(jnp.int32, x.shape, 1)
    return jnp.where((lane < HD) == (head == 0), x, jnp.zeros_like(x))


def transposed(x):
    return x.astype(jnp.float32).T.astype(x.dtype)


def causal_exp(scores, row_block, block):
    e = jnp.exp(scores)
    if row_block:
        done = e[: row_block * block]
    last = e[row_block * block :]
    key = lax.broadcasted_iota(jnp.int32, last.shape, 0)
    query = lax.broadcasted_iota(jnp.int32, last.shape, 1)
    last = jnp.where(key <= query, last, 0.0)
    return jnp.concatenate([done, last], axis=0) if row_block else last


def attend_kernel(block, mq, mk, mv, cos_ref, minus_ref, plus_ref, q_out, k_out, v_out, o_out):
    shape = q_out.shape
    length = shape[0] * shape[2]
    tabs = (cos_ref[...], minus_ref[...], plus_ref[...])
    q = rotate(mq[...].reshape(length, PAIR), *tabs).astype(jnp.bfloat16)
    k = rotate(mk[...].reshape(length, PAIR), *tabs).astype(jnp.bfloat16)
    v = mv[...].reshape(length, PAIR).astype(jnp.bfloat16)
    q_out[...] = q.reshape(shape)
    k_out[...] = k.reshape(shape)
    v_out[...] = v.reshape(shape)
    qs = q * jnp.bfloat16(HD**-0.5)
    vt = transposed(v)
    q_heads = [head_lanes(qs, h) for h in range(2)]
    rows = []
    for i in range(length // block):
        n = (i + 1) * block
        both = []
        for h in range(2):
            e = causal_exp(nt(k[:n], q_heads[h][i * block : n]), i, block)
            inv = 1.0 / jnp.sum(e, axis=0, keepdims=True)
            p = (e * inv).astype(jnp.bfloat16)
            both.append(nn(vt[h * HD : (h + 1) * HD, :n], p))
        rows.append(jnp.concatenate(both, axis=0).T)
    o_out[...] = jnp.concatenate(rows, axis=0).astype(jnp.bfloat16).reshape(shape)


def attend_back_kernel(block, q_ref, k_ref, v_ref, do_ref, cos_ref, minus_ref, plus_ref,
                       dq_out, dk_out, dv_out, dk_acc, dv_acc):
    shape = dq_out.shape
    length = shape[0] * shape[2]
    tabs = (cos_ref[...], -minus_ref[...], -plus_ref[...])
    scale = HD**-0.5
    q = q_ref[...].reshape(length, PAIR) * jnp.bfloat16(scale)
    k = k_ref[...].reshape(length, PAIR)
    v = v_ref[...].reshape(length, PAIR)
    do = do_ref[...].reshape(length, PAIR)
    kt = transposed(k)
    q_heads = [head_lanes(q, h) for h in range(2)]
    do_heads = [head_lanes(do, h) for h in range(2)]
    dk_acc[...] = jnp.zeros_like(dk_acc)
    dv_acc[...] = jnp.zeros_like(dv_acc)
    rows = []
    for i in range(length // block):
        n = (i + 1) * block
        both = []
        for h in range(2):
            q_i = q_heads[h][i * block : n]
            do_i = do_heads[h][i * block : n]
            e = causal_exp(nt(k[:n], q_i), i, block)
            p = e * (1.0 / jnp.sum(e, axis=0, keepdims=True))
            dp = nt(v[:n], do_i)
            inner = jnp.sum(p * dp, axis=0, keepdims=True)
            ds = (p * (dp - inner)).astype(jnp.bfloat16)
            dv_acc[:n] += nn(p.astype(jnp.bfloat16), do_i)
            dk_acc[:n] += nn(ds, q_i)
            both.append(nn(kt[h * HD : (h + 1) * HD, :n], ds))
        rows.append(jnp.concatenate(both, axis=0).T)

    def finish(g):
        return g.astype(jnp.bfloat16).astype(jnp.float32)

    dq = finish(jnp.concatenate(rows, axis=0) * scale)
    dq_out[...] = rotate(dq, *tabs).astype(jnp.bfloat16).reshape(shape)
    dk_out[...] = rotate(finish(dk_acc[...]), *tabs).astype(jnp.bfloat16).reshape(shape)
    dv_out[...] = dv_acc[...].astype(jnp.bfloat16).reshape(shape)


def attention_specs(parts, seqs, local_len, width):
    pairs = width // PAIR

    def spec(offset):
        return pl.BlockSpec((parts, 1, local_len, PAIR), lambda i, j: (0, i, 0, offset * pairs + j))

    length = parts * local_len
    tab = pl.BlockSpec((length, PAIR), lambda i, j: (0, 0))
    return spec, tab, (seqs, pairs), min(256, length)


def attend(m, tabs, width):
    parts, seqs, local_len, _ = m.shape
    spec, tab, grid, block = attention_specs(parts, seqs, local_len, width)
    out = jax.ShapeDtypeStruct((parts, seqs, local_len, width), jnp.bfloat16)
    work = seqs * (width // HD) * (parts * local_len) ** 2
    return pl.pallas_call(
        functools.partial(attend_kernel, block),
        grid=grid,
        in_specs=[spec(0), spec(1), spec(2), tab, tab, tab],
        out_specs=[spec(0)] * 4,
        out_shape=[out] * 4,
        compiler_params=pltpu.CompilerParams(vmem_limit_bytes=48 << 20),
        cost_estimate=pl.CostEstimate(
            flops=work * HD * 4, bytes_accessed=m.size * 4 + out.size * 8, transcendentals=work
        ),
        name="attend",
    )(m, m, m, *tabs)


def attend_back(q, k, v, do, tabs):
    parts, seqs, local_len, width = q.shape
    spec, tab, grid, block = attention_specs(parts, seqs, local_len, width)
    out = jax.ShapeDtypeStruct(q.shape, jnp.bfloat16)
    length = parts * local_len
    work = seqs * (width // HD) * length**2
    return pl.pallas_call(
        functools.partial(attend_back_kernel, block),
        grid=grid,
        in_specs=[spec(0)] * 4 + [tab] * 3,
        out_specs=[spec(0)] * 3,
        out_shape=[out] * 3,
        scratch_shapes=[pltpu.VMEM((length, PAIR), jnp.float32)] * 2,
        compiler_params=pltpu.CompilerParams(vmem_limit_bytes=48 << 20),
        cost_estimate=pl.CostEstimate(
            flops=work * HD * 10, bytes_accessed=out.size * 14, transcendentals=work
        ),
        name="attend_back",
    )(q, k, v, do, *tabs)


def mid_kernel(core_ref, o_ref, mine_ref, other_ref, x_ref, gain_ref, shift_ref, x1_out, a_out):
    step = pl.program_id(0)
    core = core_ref[0]

    @pl.when(step == 0)
    def _():
        x1_out[...] = x_ref[...].astype(jnp.float32)

    x1_out[...] += nn(o_ref[core], mine_ref[0]) + nn(o_ref[1 - core], other_ref[0])

    @pl.when(step == pl.num_programs(0) - 1)
    def _():
        xh, _ = norm_stats(x1_out[...])
        a_out[...] = (xh * gain_ref[...] + shift_ref[...]).astype(jnp.bfloat16)


def mid(core, o, mine, other, x, gain, shift):
    parts, rows, head_width = o.shape
    width = x.shape[1]
    whole = lambda shape: pl.BlockSpec(shape, lambda i, c: (0, 0))
    return pl.pallas_call(
        mid_kernel,
        grid_spec=pltpu.PrefetchScalarGridSpec(
            num_scalar_prefetch=1,
            grid=(parts // 2,),
            in_specs=[
                pl.BlockSpec((2, rows, head_width), lambda i, c: (i, 0, 0)),
                pl.BlockSpec((1, head_width, width), lambda i, c: (i, 0, 0)),
                pl.BlockSpec((1, head_width, width), lambda i, c: (i, 0, 0)),
                whole((rows, width)),
                whole((1, width)),
                whole((1, width)),
            ],
            out_specs=[whole((rows, width)), whole((rows, width))],
        ),
        out_shape=[
            jax.ShapeDtypeStruct((rows, width), jnp.float32),
            jax.ShapeDtypeStruct((rows, width), jnp.bfloat16),
        ],
        compiler_params=pltpu.CompilerParams(vmem_limit_bytes=48 << 20),
        cost_estimate=pl.CostEstimate(
            flops=2 * rows * width * width,
            bytes_accessed=2 * width * width + 10 * rows * width,
            transcendentals=0,
        ),
        name="mid",
    )(core, o, mine, other, x, gain[None, :], shift[None, :])


def mid_back_kernel(count, core_ref, *refs):
    pieces = refs[:count]
    x1_ref, dy_ref, gain_ref, mine_ref, other_ref = refs[count : count + 5]
    dx1_out, dxl_out, do_out, gain_out, shift_out = refs[count + 5 :]
    core = core_ref[0]

    @pl.when(pl.program_id(0) == 0)
    def _():
        dn = pieces[0][...].astype(jnp.float32)
        for piece in pieces[1:]:
            dn = dn + piece[...].astype(jnp.float32)
        xh, r = norm_stats(x1_ref[...])
        gain_out[...] = jnp.sum(dn * xh, axis=0, keepdims=True)
        shift_out[...] = jnp.sum(dn, axis=0, keepdims=True)
        dx1 = dy_ref[...].astype(jnp.float32) + norm_back(dn, xh, r, gain_ref[...])
        dx1_out[...] = dx1
        dxl_out[...] = dx1.astype(jnp.bfloat16)

    dxl = dxl_out[...]
    do_out[core] = nt(dxl, mine_ref[0]).astype(jnp.bfloat16)
    do_out[1 - core] = nt(dxl, other_ref[0]).astype(jnp.bfloat16)


def mid_back(core, pieces, x1, dy, gain, mine, other):
    rows, width = x1.shape
    halves, head_width, _ = mine.shape
    whole = lambda shape: pl.BlockSpec(shape, lambda i, c: (0, 0))
    full = whole((rows, width))
    weight = pl.BlockSpec((1, head_width, width), lambda i, c: (i, 0, 0))
    return pl.pallas_call(
        functools.partial(mid_back_kernel, len(pieces)),
        grid_spec=pltpu.PrefetchScalarGridSpec(
            num_scalar_prefetch=1,
            grid=(halves,),
            in_specs=[full] * (len(pieces) + 2) + [whole((1, width)), weight, weight],
            out_specs=[
                full,
                full,
                pl.BlockSpec((2, rows, head_width), lambda i, c: (i, 0, 0)),
                whole((1, width)),
                whole((1, width)),
            ],
        ),
        out_shape=[
            jax.ShapeDtypeStruct((rows, width), jnp.float32),
            jax.ShapeDtypeStruct((rows, width), jnp.bfloat16),
            jax.ShapeDtypeStruct((2 * halves, rows, head_width), jnp.bfloat16),
            jax.ShapeDtypeStruct((1, width), jnp.float32),
            jax.ShapeDtypeStruct((1, width), jnp.float32),
        ],
        compiler_params=pltpu.CompilerParams(vmem_limit_bytes=56 << 20),
        cost_estimate=pl.CostEstimate(
            flops=2 * rows * width * width,
            bytes_accessed=2 * width * width + 20 * rows * width,
            transcendentals=0,
        ),
        name="mid_back",
    )(core, *pieces, x1, dy, gain[None, :], mine, other)


def joint_kernel(count, *refs):
    dq_ref, dk_ref, dv_ref, w_ref = refs[:4]
    x_refs = refs[4 : 4 + count]
    o_refs = refs[4 + count : 4 + 2 * count]
    out_ref = refs[-1]
    width, cols = w_ref.shape
    part = cols // 3
    w = w_ref[...]
    total = nt(dq_ref[...], w[:, :part])
    total = total + nt(dk_ref[...], w[:, part : 2 * part])
    total = total + nt(dv_ref[...], w[:, 2 * part :])
    out_ref[:, :width] = total.astype(jnp.bfloat16)
    for h in range(2):
        side = tn(x_refs[0][...], o_refs[0][h])
        for x_ref, o_ref in zip(x_refs[1:], o_refs[1:]):
            side = side + tn(x_ref[...], o_ref[h])
        start = width + h * part
        out_ref[:, start : start + part] = side.astype(jnp.bfloat16)


def joint(dq, dk, dv, w, xs, os):
    all_rows, part = dq.shape
    width, cols = w.shape
    rows = xs[0].shape[0]
    count = len(xs)
    parts = width // part
    block = all_rows // parts
    if block != part:
        raise ValueError("unsupported shape")
    row_block = pl.BlockSpec((block, part), lambda i: (i, 0))
    return pl.pallas_call(
        functools.partial(joint_kernel, count),
        grid=(parts,),
        in_specs=[row_block] * 3
        + [pl.BlockSpec((width, cols), lambda i: (0, 0))]
        + [pl.BlockSpec((rows, part), lambda i: (0, i))] * count
        + [pl.BlockSpec((2, rows, part), lambda i: (0, 0, 0))] * count,
        out_specs=pl.BlockSpec((block, width + 2 * part), lambda i: (i, 0)),
        out_shape=jax.ShapeDtypeStruct((all_rows, width + 2 * part), jnp.bfloat16),
        compiler_params=pltpu.CompilerParams(vmem_limit_bytes=48 << 20),
        cost_estimate=pl.CostEstimate(
            flops=2 * all_rows * width * cols + 4 * count * rows * width * part,
            bytes_accessed=4 * all_rows * (width + cols) + 2 * width * cols,
            transcendentals=0,
        ),
        name="joint",
    )(dq, dk, dv, w, *xs, *os)


def pick_kernel(counts, core_ref, gate_ref, up_ref, out_ref):
    blocks, fsdp_parts, part = counts

    def pick(source):
        rows = source[...]
        for f in range(fsdp_parts):
            starts = [(t * fsdp_parts + f) * part for t in range(blocks)]
            out_ref[f] = jnp.concatenate([rows[:, a : a + part] for a in starts], axis=1)

    @pl.when(core_ref[0] == 0)
    def _():
        pick(gate_ref)

    @pl.when(core_ref[0] != 0)
    def _():
        pick(up_ref)


def pick(core, gate, up, blocks, fsdp_parts):
    rows, cols = gate.shape
    part = cols // (blocks * fsdp_parts)
    block = min(64, rows)
    return pl.pallas_call(
        functools.partial(pick_kernel, (blocks, fsdp_parts, part)),
        grid_spec=pltpu.PrefetchScalarGridSpec(
            num_scalar_prefetch=1,
            grid=(rows // block,),
            in_specs=[
                pl.BlockSpec((block, cols), lambda i, c: (jnp.where(c[0] == 0, i, 0), 0)),
                pl.BlockSpec((block, cols), lambda i, c: (jnp.where(c[0] == 0, 0, i), 0)),
            ],
            out_specs=pl.BlockSpec((fsdp_parts, block, blocks * part), lambda i, c: (0, i, 0)),
        ),
        out_shape=jax.ShapeDtypeStruct((fsdp_parts, rows, blocks * part), gate.dtype),
        compiler_params=pltpu.CompilerParams(vmem_limit_bytes=32 << 20),
        cost_estimate=pl.CostEstimate(flops=0, bytes_accessed=4 * rows * cols, transcendentals=0),
        name="pick",
    )(core, gate, up)


def third_rounds(parts):
    left = {s: [(j, (j * parts + s) // 3, (j * parts + s) % 3) for j in range(3)] for s in range(parts)}
    rounds = []
    for _ in range(3):
        owner = {}

        def place(s, seen):
            for edge in left[s]:
                d = edge[1]
                if d in seen:
                    continue
                seen.add(d)
                if d not in owner or place(owner[d][0], seen):
                    owner[d] = (s, edge)
                    return True
            return False

        for s in range(parts):
            place(s, set())
        send = [0] * parts
        slot = [0] * parts
        pairs = []
        for d, (s, edge) in owner.items():
            left[s].remove(edge)
            send[s] = edge[0]
            slot[d] = edge[2]
            pairs.append((s, d))
        rounds.append((sorted(pairs), send, slot))
    return rounds


def contiguous_thirds(block, parts, me):
    got = []
    slots = []
    for pairs, send, slot in third_rounds(parts):
        piece = lax.dynamic_index_in_dim(block, jnp.array(send)[me], 1, keepdims=False)
        got.append(lax.ppermute(piece, "seq", pairs))
        slots.append(jnp.array(slot)[me])
    out = []
    for k in range(3):
        out.append(jnp.where(slots[0] == k, got[0], jnp.where(slots[1] == k, got[1], got[2])))
    return jnp.concatenate(out, axis=1)


def after(x, *done):
    return lax.optimization_barrier((x, *done))[0]


def flip_pairs(parts, j):
    return [(i, i ^ j) for i in range(parts)]


def gather_flips(block, parts):
    return [block] + [lax.ppermute(block, "fsdp", flip_pairs(parts, j)) for j in range(1, parts)]


def relay_near(block, parts):
    if parts != 4:
        return gather_flips(block, parts)[1:]
    return [lax.ppermute(block, "fsdp", flip_pairs(parts, j)) for j in (1, 2)]


def relay_halves(near, parts):
    if parts != 4:
        return []
    one, two = near
    half = one.shape[0] // 2
    return [two[:half], one[half:]]


def relay_far(block, near, halves):
    if not halves:
        return [block, *near]
    got = [lax.ppermute(halves[j - 1], "fsdp", flip_pairs(4, j)) for j in (1, 2)]
    return [block, *near, tuple(got)]


def send_flips(pieces, parts):
    return [pieces[0]] + [
        lax.ppermute(pieces[j], "fsdp", flip_pairs(parts, j)) for j in range(1, parts)
    ]


def total(pieces):
    out = pieces[0].astype(jnp.float32)
    for piece in pieces[1:]:
        out = out + piece.astype(jnp.float32)
    return out


def project_kernel(x_ref, gain_ref, shift_ref, w_ref, bias_ref, m_out, a_out):
    x = x_ref[...].astype(jnp.float32)
    xh, _ = norm_stats(x)
    a = (xh * gain_ref[...] + shift_ref[...]).astype(jnp.bfloat16)
    a_out[...] = a
    m_out[...] = nn(a, w_ref[...]) + bias_ref[...]


def project(x, gain, shift, w, bias):
    rows, width = x.shape
    cols = w.shape[1]
    block = min(256, rows)
    whole = lambda shape: pl.BlockSpec(shape, lambda i: (0, 0))
    return pl.pallas_call(
        project_kernel,
        grid=(rows // block,),
        in_specs=[
            pl.BlockSpec((block, width), lambda i: (i, 0)),
            whole((1, width)),
            whole((1, width)),
            whole((width, cols)),
            whole((1, cols)),
        ],
        out_specs=[
            pl.BlockSpec((block, cols), lambda i: (i, 0)),
            pl.BlockSpec((block, width), lambda i: (i, 0)),
        ],
        out_shape=[
            jax.ShapeDtypeStruct((rows, cols), jnp.float32),
            jax.ShapeDtypeStruct((rows, width), jnp.bfloat16),
        ],
        compiler_params=pltpu.CompilerParams(vmem_limit_bytes=48 << 20),
        cost_estimate=pl.CostEstimate(
            flops=2 * rows * width * cols,
            bytes_accessed=rows * width * 4 + rows * cols * 4 + width * cols * 2,
            transcendentals=0,
        ),
        name="project",
    )(x, gain[None, :], shift[None, :], w, bias[None, :])


def to_rows(block, fsdp_parts, here):
    rows = block.shape[2] // fsdp_parts
    pieces = []
    for j in range(fsdp_parts):
        piece = lax.dynamic_slice_in_dim(block, (here ^ j) * rows, rows, 2)
        pieces.append(lax.ppermute(piece, "fsdp", flip_pairs(fsdp_parts, j)) if j else piece)
    return pieces


def on_device(
    tokens,
    attn_gain,
    attn_shift,
    qkv_weight,
    qkv_bias,
    out_weight,
    ffn_gain,
    ffn_shift,
    gate_weight,
    up_weight,
    down_weight,
    cotangent,
):
    f32, bf16 = jnp.float32, jnp.bfloat16
    seqs, local_len, width = tokens.shape
    S = lax.axis_size("seq")
    F = lax.axis_size("fsdp")
    me = lax.axis_index("seq")
    devices = S * F
    rows = seqs * local_len
    all_rows = S * rows
    head_width = width // S
    ff_rows, _ = down_weight.shape
    shard = width // F

    ratio = S // F
    if ratio != 2 or F & (F - 1):
        raise ValueError("unsupported mesh")
    ff_block = F * ff_rows // S
    ff_part = ff_block // F
    even = me % 2 == 0
    core = (me % 2).reshape(1).astype(jnp.int32)
    mate = flip_pairs(S, 1)
    here = lax.axis_index("fsdp")

    def natural(pieces):
        out = jnp.zeros((F, *pieces[0].shape), pieces[0].dtype)
        rest = (0,) * (pieces[0].ndim - 1)
        for j, piece in enumerate(pieces):
            start = 0
            for part in piece if isinstance(piece, tuple) else (piece,):
                out = lax.dynamic_update_slice(out, part[None], (here ^ j, start, *rest))
                start += part.shape[0]
        return out

    x_all = lax.all_gather(tokens, "seq", axis=0).reshape(all_rows, width)
    small = jnp.concatenate([attn_gain, attn_shift, ffn_gain, ffn_shift, qkv_bias])
    small = natural(gather_flips(small, F))
    params = [small[:, i * shard : (i + 1) * shard].reshape(width).astype(f32) for i in range(4)]
    gain1, shift1, gain2, shift2 = params
    bias = small[:, 4 * shard :].reshape(3, S, head_width).astype(f32)
    bias = lax.dynamic_index_in_dim(bias, me, 1, keepdims=False).reshape(3 * head_width)
    qkv_part = jnp.concatenate(
        [
            lax.dynamic_slice_in_dim(qkv_weight, j * width + me * head_width, head_width, 1)
            for j in range(3)
        ],
        axis=1,
    )
    qkv_near = relay_near(qkv_part, F)
    qkv_got = relay_far(qkv_part, qkv_near, relay_halves(qkv_near, F))
    w_qkv = natural(qkv_got).reshape(width, 3 * head_width)

    out_half = lax.dynamic_slice_in_dim(out_weight, me % 2 * head_width, head_width, 0)
    out_mine = lax.all_gather(out_half, "fsdp", axis=0)
    fetched = after(pick(core, gate_weight, up_weight, S, F), qkv_near)
    w_mine = lax.all_to_all(fetched, "fsdp", split_axis=0, concat_axis=0, tiled=True)
    w_mine = w_mine.reshape(width, ff_rows)
    w_other = lax.ppermute(w_mine, "seq", mate)

    tabs = rotary_tables(S * local_len)
    m, a1 = project(x_all, gain1, shift1, w_qkv, bias)
    q, k, v, o = attend(m.reshape(S, seqs, local_len, 3 * head_width), tabs, head_width)
    o_got = lax.all_to_all(o, "seq", split_axis=0, concat_axis=0, tiled=True)
    dy_own = cotangent.reshape(rows, width)
    dy_near = relay_near(after(dy_own, o), F)
    out_other = lax.ppermute(out_mine, "seq", mate)
    o_got = o_got.reshape(S, rows, head_width)

    x_own = tokens.reshape(rows, width)
    x1, a2 = mid(core, o_got, out_mine, out_other, x_own, gain2, shift2)
    a2_near = relay_near(a2, F)
    a2_got = relay_far(a2, a2_near, relay_halves(a2_near, F))
    dy_halves = relay_halves(dy_near, F)
    a2_got[-1], dy_halves = after((a2_got[-1], dy_halves), dy_halves)
    a2_all = natural(a2_got).reshape(F * rows, width)
    dy_got = relay_far(dy_own, dy_near, after(dy_halves, a2_all))
    first = nn(a2_all, w_mine)
    dy_all = natural(dy_got).reshape(F * rows, width)
    down_half = lax.dynamic_index_in_dim(
        down_weight.reshape(ratio, F, ff_part, width), me % 2, 0, keepdims=False
    )
    down_half = after(down_half, first)
    down_mine = lax.all_to_all(down_half, "fsdp", split_axis=0, concat_axis=0, tiled=True)
    down_other = lax.ppermute(down_mine, "seq", mate)
    second = nn(a2_all, w_other)
    g = jnp.where(even, first, second)
    u = jnp.where(even, second, first)
    sig = jax.nn.sigmoid(g)
    silu = g * sig
    hid = (silu * u).astype(bf16)
    down_grad_part = tn(hid, dy_all).astype(bf16)
    down_grad = lax.psum_scatter(down_grad_part, "seq", scatter_dimension=1, tiled=True)
    down_mine, down_other, dy_late = after((down_mine, down_other, dy_all), down_grad_part)
    w_down = jnp.stack(
        [jnp.where(even, down_mine, down_other), jnp.where(even, down_other, down_mine)], axis=1
    ).reshape(ff_rows, width)
    dh = nt(dy_late, w_down)
    dg = (dh * u * sig * (1.0 + g * (1.0 - sig))).astype(bf16)
    du = (dh * silu).astype(bf16)
    d_first = jnp.where(even, dg, du)
    d_second = jnp.where(even, du, dg)
    dn2_part = (nt(d_first, w_mine) + nt(d_second, w_other)).astype(bf16)
    dn2_part = dn2_part.reshape(F, rows, width)
    dn2_pieces = [
        lax.dynamic_index_in_dim(dn2_part, here ^ j, 0, keepdims=False) for j in range(F)
    ]
    dgu = after(jnp.concatenate([dg, du], axis=1), dn2_pieces)
    dn2_pieces = send_flips(dn2_pieces, F)
    both_part = tn(dgu, a2_all).astype(bf16)
    both_part = both_part.reshape(2, ff_rows, width)
    both = lax.psum_scatter(both_part, "seq", scatter_dimension=1, tiled=True)
    hid_late = after(hid, both_part)
    down_part = nn(hid_late, w_down).astype(bf16).reshape(F, rows, width)
    down_out = [lax.dynamic_index_in_dim(down_part, here ^ j, 0, keepdims=False) for j in range(F)]

    dn2_pieces = after(dn2_pieces, down_out)
    dx1, dxl, do_two, gain2_part, shift2_part = mid_back(
        core, dn2_pieces, x1, dy_own, gain2, out_mine, out_other
    )
    do = lax.all_to_all(do_two, "seq", split_axis=0, concat_axis=0, tiled=True)
    do = do.reshape(S, seqs, local_len, head_width)

    dxl_pieces = gather_flips(dxl, F)
    o_got = after(o_got, dxl)
    o_pieces = []
    for j in range(F):
        piece = lax.dynamic_slice_in_dim(o_got, 2 * (here ^ j), 2, 0)
        o_pieces.append(lax.ppermute(piece, "fsdp", flip_pairs(F, j)) if j else piece)

    dm_parts = [g.reshape(all_rows, head_width) for g in attend_back(q, k, v, do, tabs)]
    down_out = after(down_out, dm_parts)
    down_pieces = send_flips(down_out, F)
    joint_part = joint(*dm_parts, w_qkv, dxl_pieces, o_pieces)
    joint_sum = lax.psum_scatter(joint_part, "seq", scatter_dimension=0, tiled=True)

    a1_late, dm_parts, both = after((a1, dm_parts, both), joint_part)
    dm = jnp.concatenate(dm_parts, axis=1)
    both_pieces = to_rows(both, F, here)
    qkv_part_grad = tn(a1_late, dm).astype(bf16)
    qkv_part_grad = qkv_part_grad.reshape(F, shard, 3 * head_width)
    qkv_pieces = [
        lax.dynamic_index_in_dim(qkv_part_grad, here ^ j, 0, keepdims=False) for j in range(F)
    ]
    down_grad = after(down_grad, qkv_pieces)
    qkv_got = send_flips(qkv_pieces, F)
    down_grad = down_grad.reshape(F, ratio * ff_part, head_width)
    down_grad_pieces = send_flips(
        [lax.dynamic_index_in_dim(down_grad, here ^ j, 0, keepdims=False) for j in range(F)], F
    )
    dm_late, dn1_late, x_late = after((dm, joint_part, x_all), qkv_pieces)
    xh_all, _ = norm_stats(x_late.astype(f32))
    dn1_late = dn1_late[:, :width].astype(f32)
    attn_gain_part = jnp.sum(dn1_late * xh_all, axis=0)
    attn_shift_part = jnp.sum(dn1_late, axis=0)
    qkv_got = after(qkv_got, attn_gain_part)
    qkv_sum = total(qkv_got).astype(bf16)
    qkv_result = contiguous_thirds(qkv_sum.reshape(shard, 3, head_width), S, me).astype(f32)
    both_pieces, down_grad_pieces, down_pieces = after(
        (both_pieces, down_grad_pieces, down_pieces), qkv_sum
    )
    both = natural(both_pieces).transpose(1, 0, 2, 3).reshape(2, ff_block, shard).astype(f32)
    gate_result, up_result = both[0].T, both[1].T
    down_result = natural(down_grad_pieces).reshape(F, ratio, ff_part, head_width)
    down_result = down_result.transpose(1, 0, 2, 3).reshape(ff_rows, head_width).astype(f32)
    layer_out = (x1 + total(down_pieces)).astype(bf16).reshape(tokens.shape)
    joint_sum = after(joint_sum, qkv_result, layer_out, gate_result, up_result, down_result)
    dn1 = joint_sum[:, :width].astype(f32)
    out_result = joint_sum[:, width:].T.astype(f32)

    bias_part = jnp.sum(dm_late, axis=0, dtype=f32).reshape(3, 1, head_width)
    bias_full = lax.dynamic_update_slice_in_dim(
        jnp.zeros((3, S, head_width), f32), bias_part, me, 1
    ).reshape(3 * width)
    small_parts = [
        attn_gain_part,
        attn_shift_part,
        bias_full[: 2 * width],
        bias_full[2 * width :],
        gain2_part[0],
        shift2_part[0],
    ]
    packed = jnp.concatenate([p.reshape(devices, -1) for p in small_parts], axis=1)
    packed = lax.all_to_all(packed, MESH_AXES, split_axis=0, concat_axis=0, tiled=True)
    xh, r = norm_stats(x_own.astype(f32))
    tokens_grad = (dx1 + norm_back(dn1, xh, r, gain1)).reshape(tokens.shape)
    packed = jnp.sum(after(packed, tokens_grad), axis=0)
    results = []
    start = 0
    for p in small_parts:
        size = p.shape[0] // devices
        results.append(packed[start : start + size])
        start += size
    gain1_result, shift1_result, bias_result, value_result, gain2_result, shift2_result = results

    return (
        layer_out,
        tokens_grad,
        gain1_result,
        shift1_result,
        qkv_result,
        bias_result,
        value_result,
        out_result,
        gain2_result,
        shift2_result,
        gate_result,
        up_result,
        down_result,
    )


def solution(mesh):
    return jax.shard_map(
        on_device,
        mesh=mesh,
        in_specs=(
            P("fsdp", "seq", None),
            P("fsdp"),
            P("fsdp"),
            P("fsdp", None),
            P("fsdp"),
            P("fsdp", None),
            P("fsdp"),
            P("fsdp"),
            P("fsdp", None),
            P("fsdp", None),
            P("fsdp", None),
            P("fsdp", "seq", None),
        ),
        out_specs=(
            P("fsdp", "seq", None),
            P("fsdp", "seq", None),
            P(("seq", "fsdp")),
            P(("seq", "fsdp")),
            P("fsdp", "seq"),
            P(("seq", "fsdp")),
            P(("seq", "fsdp")),
            P("fsdp", "seq"),
            P(("seq", "fsdp")),
            P(("seq", "fsdp")),
            P("fsdp", "seq"),
            P("fsdp", "seq"),
            P("fsdp", "seq"),
        ),
        check_vma=False,
    )
```
